512 devices in a mesh: var: 128 (over y, x, z_lo, core), samp: 4 (over z_hi).
Axes of the slice: x: 4, y: 4, z: 16 (z_hi: 4, z_lo: 4; z = z_hi * 4 + z_lo), core: 2. Of those that a mesh axis runs over, the one named last changes fastest.
Arguments:
- dosages: int32 [1024, 131072], P('samp', 'var'), may hold values from 0 to 3, as said below
- weights: bfloat16 [131072, 2560], P(('var', 'samp')), may hold values from -0.0625 to 0.0625
- variant_pass: int32 [131072], P('var'), may hold values 0 or 1
- ancestry: float32 [1024, 20], P('samp')
Outputs:
- standardized: float32 [2560, 1024], P('var', 'samp')
The draws below stay inside these ranges and needn't reach their ends.
Inputs may be any that keep to these rules, and one draw needn't show every extreme that they name: 3 marks a missing call; other values are allele dosages.
All inputs are finite; a program needn't handle non-finite values. No bound on the sum of `variant_pass` on one device may be relied on, other than what follows from the above.
Results may differ from the reference program's by a relative error of at most 0.0024.
Values may be sent and summed in bfloat16 or wider, within the bound.
A program may use at most 64 MiB of HBM per device.

```python
import math
import jax
import jax.numpy as jnp
from jax import lax

SCORES = 2560
COMPONENTS = 20
SAMPLES = 1024
VARIANTS = 131072


def draw_dosages(key, part):
    keys = jax.random.split(key, 6)
    base = jax.random.randint(keys[0], (VARIANTS,), 8, 57)
    leaning = jax.random.randint(keys[1], (VARIANTS,), 0, 2) * 2 - 1
    missing_base = jax.random.randint(keys[2], (VARIANTS,), 2, 9)
    position = jnp.arange(SAMPLES, dtype=jnp.int32)
    drift = position * 40 // SAMPLES - 20
    chance = jnp.clip(base[None, :] + drift[:, None] * leaning[None, :], 2, 62)
    first = jax.random.randint(keys[3], (SAMPLES, VARIANTS), 0, 64)
    second = jax.random.randint(keys[4], (SAMPLES, VARIANTS), 0, 64)
    third = jax.random.randint(keys[5], (SAMPLES, VARIANTS), 0, 64)
    dosage = (first < chance).astype(jnp.int32) + (second < chance).astype(jnp.int32)
    missing_limit = missing_base[None, :] + (position * 24 // SAMPLES)[:, None]
    return jnp.where(third < missing_limit, 3, dosage).astype(jnp.int32)


def draw_ancestry(key, part):
    keys = jax.random.split(key, 2)
    position = jnp.arange(SAMPLES, dtype=jnp.float32) * (2.0 / (SAMPLES - 1)) - 1.0
    leaning = jax.random.uniform(keys[0], (COMPONENTS,), jnp.float32, -1.2, 1.2)
    noise = jax.random.normal(keys[1], (SAMPLES, COMPONENTS), jnp.float32)
    return (noise + position[:, None] * leaning[None, :]).astype(jnp.float32)


def place_ends(array, key, least, top_value):
    longest = array.shape.index(max(array.shape))
    spots = []
    for shift in (0, 1):
        where = [jax.random.randint(jax.random.fold_in(key, axis), (), 0, length) for axis, length in enumerate(array.shape)]
        where[longest] = (where[longest] + shift) % array.shape[longest]
        spots.append(tuple(where))
    return array.at[spots[0]].set(least).at[spots[1]].set(top_value)


def spiked(array, stream_key, source, target, parts, factor):
    owner, partner = [(jnp.arange(array.shape[axis_at]) // (array.shape[axis_at] // parts)).reshape([-1 if axis == axis_at else 1 for axis in range(array.ndim)]) for axis_at in (source, target)]
    chosen = jax.random.permutation(stream_key, parts)[partner]
    strong = (owner == chosen) | (owner == (partner + parts // 2) % parts)
    return jnp.where(strong, factor * array, array)


def levels(rng, extent, shards, smallest, largest):
    gain = 1.0
    for dim, blocks in shards:
        heights = jax.random.uniform(jax.random.fold_in(jax.random.fold_in(rng, 6), dim), (blocks,), jnp.float32, smallest / len(shards), largest / len(shards))
        gain = gain * jnp.repeat(jnp.exp(heights), extent[dim] // blocks).reshape((-1,) + (1,) * (len(extent) - 1 - dim))
    return gain


def noise_with(key, shape, scale, bound, shards, heavy, kind=jnp.bfloat16):
    array = scale * jax.random.normal(key, shape, jnp.float32)
    if shards:
        array = array * levels(key, shape, shards, -0.22, 0.18)
    return jnp.clip(spiked(array, jax.random.fold_in(key, 3), *heavy), -bound, bound).astype(kind)


def setup_inputs(seed: int = 0) -> dict:
    streams_of = jax.random.split(jax.random.key(seed), 5)
    dosages = draw_dosages(jax.random.fold_in(streams_of[4], 71), 0)
    weights = noise_with(streams_of[1], (VARIANTS, SCORES), VARIANTS ** -0.5, 0.0625, ((0, 512),), (0, 1, 512, 6.0))
    variant_pass = place_ends((jax.random.randint(streams_of[2], (VARIANTS,), 0, 8) < 7).astype(jnp.int32), jax.random.fold_in(streams_of[2], 1), 0, 1)
    ancestry = draw_ancestry(jax.random.fold_in(streams_of[4], 71), 0)
    return dict(dosages=dosages, weights=weights, variant_pass=variant_pass, ancestry=ancestry)


def cholesky_apply(gram, cross):
    factor = jnp.linalg.cholesky(gram)
    order_n = gram.shape[0]
    forward = []
    for row_idx in range(order_n):
        running = cross[:, row_idx]
        for col_idx in range(row_idx):
            running = running - factor[row_idx, col_idx] * forward[col_idx]
        forward.append(running / factor[row_idx, row_idx])
    solved = [None] * order_n
    for row_idx in reversed(range(order_n)):
        running = forward[row_idx]
        for col_idx in range(row_idx + 1, order_n):
            running = running - factor[col_idx, row_idx] * solved[col_idx]
        solved[row_idx] = running / factor[row_idx, row_idx]
    return jnp.stack(solved, axis=1)

def reference(dosages, weights, variant_pass, ancestry):
    observed = dosages < 3
    allele_total = lax.optimization_barrier(jnp.sum(jnp.where(observed, dosages, 0).astype(jnp.float32), axis=0))
    observed_count = lax.optimization_barrier(jnp.sum(observed.astype(jnp.float32), axis=0))
    impute = ((allele_total + 1.0) / (observed_count + 1.0)).astype(jnp.bfloat16)
    block_size = math.gcd(VARIANTS, 8192)
    blocks = VARIANTS // block_size
    dose_blocks = dosages.reshape(SAMPLES, blocks, block_size).transpose(1, 0, 2)
    weight_blocks = weights.reshape(blocks, block_size, SCORES)
    impute_blocks = impute.reshape(blocks, block_size)
    pass_blocks = variant_pass.reshape(blocks, block_size)

    def accumulate(total, items):
        dose_piece, weight_piece, impute_piece, pass_piece = items
        genotypes = jnp.where(dose_piece < 3, dose_piece.astype(jnp.bfloat16), impute_piece[None, :])
        genotypes = genotypes * pass_piece.astype(jnp.bfloat16)[None, :]
        term = lax.dot_general(weight_piece.astype(jnp.float32), genotypes.astype(jnp.float32), (((0,), (1,)), ((), ())), precision=lax.Precision.HIGHEST)
        return (total + term, None)
    raw_scores, _ = lax.scan(accumulate, jnp.zeros((SCORES, SAMPLES), jnp.float32), (dose_blocks, weight_blocks, impute_blocks, pass_blocks))
    design = jnp.concatenate([jnp.ones((SAMPLES, 1), jnp.float32), ancestry], axis=1)
    gram = jnp.dot(design.T, design, precision=lax.Precision.HIGHEST)
    cross = jnp.dot(raw_scores, design, precision=lax.Precision.HIGHEST)
    coeffs = cholesky_apply(gram, cross)
    residual = raw_scores - jnp.dot(coeffs, design.T, precision=lax.Precision.HIGHEST)
    spread = lax.optimization_barrier(jnp.sum(residual * residual, axis=1)) / (SAMPLES - 1)
    return residual / jnp.sqrt(spread + 1e-06)[:, None]
```

```python
import jax
import jax.numpy as jnp
from jax import lax
from jax.experimental import pallas as pl
from jax.experimental.pallas import tpu as pltpu
from jax.sharding import PartitionSpec as P

F32 = jnp.float32
BF16 = jnp.bfloat16
HI = lax.Precision.HIGHEST
OFFSETS = (0, 1, 3, 2)
LANES_TO_LANES = (((1,), (1,)), ((), ()))


def inverse_factor(gram):
    rows = lax.broadcasted_iota(jnp.int32, gram.shape, 0)
    lanes = lax.broadcasted_iota(jnp.int32, gram.shape, 1)
    work = jnp.where(lanes < 21, gram, 0.0) + jnp.where(lanes == rows + 64, 1.0, 0.0)
    for k in range(21):
        scale = 1.0 / jnp.sqrt(work[k : k + 1, k : k + 1])
        row = work[k : k + 1, :] * scale
        column = work[:, k : k + 1] * scale
        work = jnp.where(rows > k, work - column * row, jnp.where(rows == k, row, work))
    return jnp.where(lanes >= 64, work, 0.0)


def kernel(
    dos_ref, w_ref, pass_ref, anc_ref, out_ref,
    wt, ds, dr, ts, tr, vec, geno, s, r, zs, zr, design, gl, gr, qt, st, sr,
    w_sem, d_send, d_recv, t_send, t_recv, g_send, g_recv, xy_send, xy_recv, z_send, z_recv,
    st_send, st_recv,
):
    v, zh = lax.axis_index("var"), lax.axis_index("samp")
    core, zl = lax.rem(v, 2), lax.rem(v // 2, 4)
    x, y = lax.rem(v // 8, 4), v // 32
    z = zh * 4 + zl
    plane = y * 4 + x

    def at(plane_to, z_to, core_to):
        return {"var": (plane_to * 4 + lax.rem(z_to, 4)) * 2 + core_to, "samp": z_to // 4}

    def remote(src, dst, send, recv, to):
        return pltpu.make_async_remote_copy(
            src_ref=src, dst_ref=dst, send_sem=send, recv_sem=recv,
            device_id=to, device_id_type=pl.DeviceIdType.MESH,
        )

    barrier = pltpu.get_barrier_semaphore()

    @pl.loop(1, 16)
    def _(step):
        pl.semaphore_signal(
            barrier, inc=1, device_id=at(lax.rem(plane + step, 16), z, core),
            device_id_type=pl.DeviceIdType.MESH,
        )

    @pl.loop(1, 32)
    def _(step):
        other = lax.rem(z * 2 + core + step, 32)
        pl.semaphore_signal(
            barrier, inc=1, device_id=at(plane, other // 2, lax.rem(other, 2)),
            device_id_type=pl.DeviceIdType.MESH,
        )

    for part in range(4):
        tile = []
        for half in range(2):
            piece = dos_ref[:, pl.ds(part * 256 + half * 128, 128)]
            seen = piece < 3
            tile.append(
                (
                    jnp.sum(jnp.where(seen, piece, 0), axis=0, keepdims=True).astype(F32),
                    jnp.sum(seen.astype(jnp.int32), axis=0, keepdims=True).astype(F32),
                )
            )
            narrow = piece.astype(F32).astype(BF16)
            for upper in range(2):
                ds[part, upper, :, pl.ds(half * 128, 128)] = narrow[upper * 128 : upper * 128 + 128]
        for half in range(2):
            ts[part, half : half + 1, :] = tile[half][0]
            ts[part, 2 + half : 3 + half, :] = tile[half][1]
            ts[part, 4 + half : 5 + half, :] = pass_ref[
                2 * part + half : 2 * part + half + 1, :
            ].astype(F32)
            ts[part, 6 + half : 7 + half, :] = jnp.zeros((1, 128), F32)
    for column in range(10):
        wt[0, pl.ds(column * 256, 256), :] = w_ref[:, pl.ds(column * 256, 256)].T
    lanes = lax.broadcasted_iota(jnp.int32, (256, 128), 1)
    design[...] = jnp.where((lanes == 20) | (lanes == 84), 1.0, 0.0)
    design[:, 0:20] = anc_ref[...]
    design[:, 64:84] = anc_ref[...]
    gl[...] = lax.dot_general(
        design[...], design[...], (((0,), (0,)), ((), ())), precision=HI,
        preferred_element_type=F32,
    )[0:24]
    dr[0, 0] = ds[zh, core]
    tr[0, 0] = ts[zh]

    pl.semaphore_wait(barrier, 46)

    def totals_copy(b, k):
        to_zh, to_core = lax.rem(zh + 4 - OFFSETS[b], 4), lax.rem(core + k, 2)
        return remote(
            ts.at[to_zh], tr.at[b, k], t_send.at[b, k], t_recv.at[b, k],
            at(plane, to_zh * 4 + zl, to_core),
        )

    def dosage_copy(b, k):
        to_zh, to_core = lax.rem(zh + 4 - OFFSETS[b], 4), lax.rem(core + k, 2)
        return remote(
            ds.at[to_zh, to_core], dr.at[b, k], d_send.at[b, k], d_recv.at[b, k],
            at(plane, to_zh * 4 + zl, to_core),
        )

    def small_copy(b, src, dst, send, recv):
        to_zh = lax.rem(zh + 4 - OFFSETS[b], 4)
        return remote(src, dst.at[b], send.at[b], recv.at[b], at(plane, to_zh * 4 + zl, core))

    def gram_copy(b):
        return small_copy(b, gl, gr, g_send, g_recv)

    def stat_copy(b):
        return small_copy(b, st, sr, st_send, st_recv)

    pieces = [(b, k) for b in (3, 1, 2, 0) for k in range(2) if b or k]
    weight_copy = remote(wt.at[0], wt.at[1], w_sem.at[0], w_sem.at[1], at(plane, z, 1 - core))
    for b, k in pieces:
        totals_copy(b, k).start()
    dosage_copy(0, 1).start()
    weight_copy.start()
    for b in (1, 2, 3):
        for k in range(2):
            dosage_copy(b, k).start()
    for b in (1, 2, 3):
        gram_copy(b).start()

    for b, k in pieces:
        totals_copy(b, k).wait_recv()
    for k in range(2):
        total = tr[0, k] + tr[1, k] + tr[2, k] + tr[3, k]
        for half in range(2):
            impute = (total[half : half + 1] + 1.0) / (total[2 + half : 3 + half] + 1.0)
            impute = impute.astype(BF16).astype(F32)
            centre = jnp.floor(impute * 4.0 + 0.5) * 0.25
            passed = tr[0, k, 4 + half : 5 + half, :]
            vec[k, half, 0:1, :] = centre
            vec[k, half, 1:2, :] = (impute - centre) * passed
            vec[k, half, 2:3, :] = passed

    def xy_copy(b, dy, dx):
        to = lax.rem(y + dy, 4) * 4 + lax.rem(x + dx, 4)
        return remote(
            s.at[b, pl.ds(to * 160, 160)], r.at[b, dy * 4 + dx],
            xy_send.at[b, dy * 4 + dx], xy_recv.at[b, dy * 4 + dx], at(to, z, core),
        )

    def multiply(b):
        for k in range(2):
            if b or k:
                dosage_copy(b, k).wait_recv()
            for half in range(2):
                dose = dr[b, k, :, pl.ds(half * 128, 128)].astype(F32)
                centre, missing = vec[k, half, 0:1, :], vec[k, half, 1:2, :]
                passed = vec[k, half, 2:3, :]
                geno[k, :, pl.ds(half * 128, 128)] = jnp.where(
                    dose < 2.5, (dose - centre) * passed, missing
                ).astype(BF16)
        if b == 0:
            weight_copy.wait_recv()

        @pl.loop(0, 4)
        def _(dy):
            rows = pl.ds(pl.multiple_of(lax.rem(y + dy, 4) * 640, 640), 640)
            s[b, rows, :] = (
                lax.dot_general(wt[0, rows, :], geno[0], LANES_TO_LANES, preferred_element_type=F32)
                + lax.dot_general(wt[1, rows, :], geno[1], LANES_TO_LANES, preferred_element_type=F32)
            ).astype(BF16)
            for dx in (1, 2, 3):
                xy_copy(b, dy, dx).start()

            @pl.when(dy > 0)
            def _():
                xy_copy(b, dy, 0).start()

    def z_copy(b, group):
        to_zh = lax.rem(zh + OFFSETS[b], 4)
        return remote(
            zs.at[b, group], zr.at[core, z], z_send.at[b, group], z_recv.at[core, z],
            at(plane, to_zh * 4 + group // 2, lax.rem(group, 2)),
        )

    mine = zl * 2 + core

    def reduce_plane(b):
        @pl.loop(1, 16)
        def _(step):
            xy_copy(b, step // 4, lax.rem(step, 4)).wait_recv()

        total = s[b, pl.ds(pl.multiple_of(plane * 160, 160), 160), :].astype(F32)
        for step in range(1, 16):
            total += r[b, step].astype(F32)
        for group in range(8):
            zs[b, group] = jnp.concatenate(
                [total[group * 20 : group * 20 + 20], jnp.zeros((4, 128), F32)], axis=0
            )
        if b == 0:
            zr[core, z] = zs[0, mine]

            @pl.loop(1, 8)
            def _(step):
                z_copy(0, lax.rem(mine + step, 8)).start()
        else:

            @pl.loop(0, 8)
            def _(step):
                z_copy(b, lax.rem(mine + step, 8)).start()

    multiply(0)
    for b in (1, 2, 3):
        gram_copy(b).wait_recv()
    inverse = inverse_factor(gl[...] + gr[1] + gr[2] + gr[3])
    qt[...] = jnp.zeros_like(qt)
    qt[0:24, :] = lax.dot_general(
        inverse, design[...], LANES_TO_LANES, precision=HI, preferred_element_type=F32
    )
    multiply(1)
    reduce_plane(0)
    multiply(2)
    reduce_plane(1)
    multiply(3)
    reduce_plane(2)
    reduce_plane(3)

    @pl.loop(1, 32)
    def _(step):
        other = lax.rem(z * 2 + core + step, 32)
        z_from, core_from = other // 2, lax.rem(other, 2)
        remote(
            zs.at[0, 0], zr.at[core_from, z_from], z_send.at[0, 0],
            z_recv.at[core_from, z_from], at(plane, z, 1 - core),
        ).wait_recv()

    raw = []
    for half in range(2):
        total = zr[half, 0]
        for source in range(1, 16):
            total += zr[half, source]
        raw.append(total)
    lane = lax.broadcasted_iota(jnp.int32, (24, 128), 1)
    cross = jnp.zeros((24, 128), F32)
    squares = jnp.zeros((24, 1), F32)
    for half in range(2):
        cross += lax.dot_general(
            raw[half], qt[:, pl.ds(half * 128, 128)], LANES_TO_LANES, precision=HI,
            preferred_element_type=F32,
        )
        squares += jnp.sum(raw[half] * raw[half], axis=1, keepdims=True)
    st[...] = jnp.where(lane == 32, squares, cross)
    for b in (3, 1, 2):
        stat_copy(b).start()
    for b in (1, 2, 3):
        stat_copy(b).wait_recv()
    stats = st[...] + sr[1] + sr[2] + sr[3]
    cross = jnp.where(lane < 24, stats, 0.0)
    squares = jnp.sum(jnp.where(lane == 32, stats, 0.0) - cross * cross, axis=1, keepdims=True)
    spread = jnp.maximum(squares, 0.0) / 1023.0
    scale = 1.0 / jnp.sqrt(spread + 1e-06)
    for half in range(2):
        fitted = jnp.dot(
            cross, qt[:, pl.ds(half * 128, 128)], precision=HI, preferred_element_type=F32
        )
        out_ref[:, pl.ds(half * 128, 128)] = ((raw[half] - fitted) * scale)[0:20]

    weight_copy.wait_send()
    for b, k in pieces:
        totals_copy(b, k).wait_send()
        dosage_copy(b, k).wait_send()
    for b in (1, 2, 3):
        gram_copy(b).wait_send()
        stat_copy(b).wait_send()
    for b in range(4):

        @pl.loop(1, 16)
        def _(step):
            xy_copy(b, step // 4, lax.rem(step, 4)).wait_send()

        @pl.loop(0 if b else 1, 8)
        def _(step):
            z_copy(b, lax.rem(mine + step, 8)).wait_send()


def on_device(dosages, weights, variant_pass, ancestry):
    dma = pltpu.SemaphoreType.DMA
    vmem = pl.BlockSpec(memory_space=pltpu.VMEM)
    return pl.pallas_call(
        kernel,
        out_shape=jax.ShapeDtypeStruct((20, 256), F32),
        in_specs=[vmem] * 4,
        out_specs=vmem,
        scratch_shapes=[
            pltpu.VMEM((2, 2560, 256), BF16),
            pltpu.VMEM((4, 2, 128, 256), BF16),
            pltpu.VMEM((4, 2, 128, 256), BF16),
            pltpu.VMEM((4, 8, 128), F32),
            pltpu.VMEM((4, 2, 8, 128), F32),
            pltpu.VMEM((2, 2, 8, 128), F32),
            pltpu.VMEM((2, 128, 256), BF16),
            pltpu.VMEM((4, 2560, 128), BF16),
            pltpu.VMEM((4, 16, 160, 128), BF16),
            pltpu.VMEM((4, 8, 24, 128), F32),
            pltpu.VMEM((2, 16, 24, 128), F32),
            pltpu.VMEM((256, 128), F32),
            pltpu.VMEM((24, 128), F32),
            pltpu.VMEM((4, 24, 128), F32),
            pltpu.VMEM((128, 256), F32),
            pltpu.VMEM((24, 128), F32),
            pltpu.VMEM((4, 24, 128), F32),
            dma((2,)),
            dma((4, 2)), dma((4, 2)), dma((4, 2)), dma((4, 2)),
            dma((4,)), dma((4,)),
            dma((4, 16)), dma((4, 16)),
            dma((4, 8)), dma((2, 16)),
            dma((4,)), dma((4,)),
        ],
        compiler_params=pltpu.CompilerParams(
            collective_id=0, has_side_effects=True, vmem_limit_bytes=40 << 20
        ),
        name="polygenic",
    )(dosages, weights, variant_pass.reshape(8, 128), ancestry)


def solution(mesh):
    in_specs = (P("samp", "var"), P(("var", "samp"), None), P("var"), P("samp", None))
    return jax.shard_map(
        on_device, mesh=mesh, in_specs=in_specs, out_specs=P("var", "samp"), check_vma=False
    )
```

```python
import jax
import jax.numpy as jnp
from jax import lax
from jax.experimental import pallas as pl
from jax.experimental.pallas import tpu as pltpu
from jax.sharding import PartitionSpec as P

F32 = jnp.float32
BF16 = jnp.bfloat16
HI = lax.Precision.HIGHEST
OFFSETS = (0, 1, 3, 2)
LANES_TO_LANES = (((1,), (1,)), ((), ()))


def pack(wide):
    return wide[0:8] + pltpu.roll(wide[8:16], 32, 1) + pltpu.roll(wide[16:24], 64, 1)


def unpack(tile):
    rows = jnp.concatenate([tile, pltpu.roll(tile, 96, 1), pltpu.roll(tile, 64, 1)], axis=0)
    return jnp.where(lax.broadcasted_iota(jnp.int32, (24, 128), 1) < 32, rows, 0.0)


def inverse_factor(gram):
    rows = lax.broadcasted_iota(jnp.int32, gram.shape, 0)
    lanes = lax.broadcasted_iota(jnp.int32, gram.shape, 1)
    work = jnp.where(lanes < 21, gram, 0.0) + jnp.where(lanes == rows + 64, 1.0, 0.0)
    for k in range(21):
        scale = 1.0 / jnp.sqrt(work[k : k + 1, k : k + 1])
        row = work[k : k + 1, :] * scale
        column = work[:, k : k + 1] * scale
        work = jnp.where(rows > k, work - column * row, jnp.where(rows == k, row, work))
    return jnp.where(lanes >= 64, work, 0.0)


def kernel(
    dos_hbm, w_hbm, pass_hbm, anc_hbm, out_ref,
    dos_ref, w_ref, pass_ref, anc_ref,
    wt, ds, dr, ts, tr, vec, geno, s, r, zs, zr, design, gl, gr, qt, st, sr,
    in_sem, w_sem, d_send, d_recv, t_send, t_recv, g_send, g_recv, xy_send, xy_recv, z_send, z_recv,
    st_send, st_recv,
):
    v, zh = lax.axis_index("var"), lax.axis_index("samp")
    core, zl = lax.rem(v, 2), lax.rem(v // 2, 4)
    x, y = lax.rem(v // 8, 4), v // 32
    z = zh * 4 + zl
    plane = y * 4 + x

    def at(plane_to, z_to, core_to):
        return {"var": (plane_to * 4 + lax.rem(z_to, 4)) * 2 + core_to, "samp": z_to // 4}

    def remote(src, dst, send, recv, to):
        return pltpu.make_async_remote_copy(
            src_ref=src, dst_ref=dst, send_sem=send, recv_sem=recv,
            device_id=to, device_id_type=pl.DeviceIdType.MESH,
        )

    loads = [
        pltpu.make_async_copy(src, dst, in_sem.at[i])
        for i, (src, dst) in enumerate(
            ((dos_hbm, dos_ref), (pass_hbm, pass_ref), (anc_hbm, anc_ref), (w_hbm, w_ref))
        )
    ]
    for load in loads:
        load.start()
    barrier = pltpu.get_barrier_semaphore()

    @pl.loop(1, 16)
    def _(step):
        pl.semaphore_signal(
            barrier, inc=1, device_id=at(lax.rem(plane + step, 16), z, core),
            device_id_type=pl.DeviceIdType.MESH,
        )

    @pl.loop(1, 32)
    def _(step):
        other = lax.rem(z * 2 + core + step, 32)
        pl.semaphore_signal(
            barrier, inc=1, device_id=at(plane, other // 2, lax.rem(other, 2)),
            device_id_type=pl.DeviceIdType.MESH,
        )

    loads[0].wait()
    loads[1].wait()
    for part in range(4):
        tile = []
        for half in range(2):
            piece = dos_ref[:, pl.ds(part * 256 + half * 128, 128)]
            seen = piece < 3
            tile.append(
                (
                    jnp.sum(jnp.where(seen, piece, 0), axis=0, keepdims=True).astype(F32),
                    jnp.sum(seen.astype(jnp.int32), axis=0, keepdims=True).astype(F32),
                )
            )
            narrow = piece.astype(F32).astype(BF16)
            for upper in range(2):
                ds[part, upper, :, pl.ds(half * 128, 128)] = narrow[upper * 128 : upper * 128 + 128]
        for half in range(2):
            ts[part, half : half + 1, :] = tile[half][0]
            ts[part, 2 + half : 3 + half, :] = tile[half][1]
            ts[part, 4 + half : 5 + half, :] = pass_ref[
                2 * part + half : 2 * part + half + 1, :
            ].astype(F32)
            ts[part, 6 + half : 7 + half, :] = jnp.zeros((1, 128), F32)
    loads[2].wait()
    design[...] = jnp.zeros_like(design)
    for row in (0, 64):
        design[row : row + 20, :] = anc_ref[...]
        design[row + 20 : row + 21, :] = jnp.ones((1, 256), F32)
    lane = lax.broadcasted_iota(jnp.int32, (24, 128), 1)
    gram = lax.dot_general(
        design[0:24, :], design[...], LANES_TO_LANES, precision=HI, preferred_element_type=F32
    )
    gl[...] = pack(jnp.where(lane < 32, gram, 0.0))
    loads[3].wait()
    for column in range(10):
        wt[0, pl.ds(column * 256, 256), :] = w_ref[:, pl.ds(column * 256, 256)].T
    dr[0, 0] = ds[zh, core]
    tr[0, 0] = ts[zh]

    pl.semaphore_wait(barrier, 46)

    def totals_copy(b, k):
        to_zh, to_core = lax.rem(zh + 4 - OFFSETS[b], 4), lax.rem(core + k, 2)
        return remote(
            ts.at[to_zh], tr.at[b, k], t_send.at[b, k], t_recv.at[b, k],
            at(plane, to_zh * 4 + zl, to_core),
        )

    def dosage_copy(b, k):
        to_zh, to_core = lax.rem(zh + 4 - OFFSETS[b], 4), lax.rem(core + k, 2)
        return remote(
            ds.at[to_zh, to_core], dr.at[b, k], d_send.at[b, k], d_recv.at[b, k],
            at(plane, to_zh * 4 + zl, to_core),
        )

    def small_copy(b, src, dst, send, recv):
        to_zh = lax.rem(zh + 4 - OFFSETS[b], 4)
        return remote(src, dst.at[b], send.at[b], recv.at[b], at(plane, to_zh * 4 + zl, core))

    def gram_copy(b):
        return small_copy(b, gl, gr, g_send, g_recv)

    def stat_copy(b):
        return small_copy(b, st, sr, st_send, st_recv)

    pieces = [(b, k) for b in (3, 1, 2, 0) for k in range(2) if b or k]
    weight_copy = remote(wt.at[0], wt.at[1], w_sem.at[0], w_sem.at[1], at(plane, z, 1 - core))
    for b, k in pieces:
        totals_copy(b, k).start()
    dosage_copy(0, 1).start()
    weight_copy.start()
    for k in range(2):
        for b in (1, 2):
            dosage_copy(b, k).start()
    for b in (1, 2, 3):
        gram_copy(b).start()

    for b, k in pieces:
        totals_copy(b, k).wait_recv()
    for k in range(2):
        total = tr[0, k] + tr[1, k] + tr[2, k] + tr[3, k]
        for half in range(2):
            impute = (total[half : half + 1] + 1.0) / (total[2 + half : 3 + half] + 1.0)
            impute = impute.astype(BF16).astype(F32)
            centre = jnp.floor(impute * 4.0 + 0.5) * 0.25
            passed = tr[0, k, 4 + half : 5 + half, :]
            vec[k, half, 0:1, :] = centre
            vec[k, half, 1:2, :] = (impute - centre) * passed
            vec[k, half, 2:3, :] = passed

    def xy_copy(b, dy, dx):
        to = lax.rem(y + dy, 4) * 4 + lax.rem(x + dx, 4)
        return remote(
            s.at[b, pl.ds(to * 160, 160)], r.at[b, dy * 4 + dx],
            xy_send.at[b, dy * 4 + dx], xy_recv.at[b, dy * 4 + dx], at(to, z, core),
        )

    def multiply(b):
        for k in range(2):
            if b or k:
                dosage_copy(b, k).wait_recv()
            for half in range(2):
                dose = dr[b, k, :, pl.ds(half * 128, 128)].astype(F32)
                centre, missing = vec[k, half, 0:1, :], vec[k, half, 1:2, :]
                passed = vec[k, half, 2:3, :]
                geno[k, :, pl.ds(half * 128, 128)] = jnp.where(
                    dose < 2.5, (dose - centre) * passed, missing
                ).astype(BF16)
        if b == 0:
            weight_copy.wait_recv()

        @pl.loop(0, 4)
        def _(dy):
            rows = pl.ds(pl.multiple_of(lax.rem(y + dy, 4) * 640, 640), 640)
            s[b, rows, :] = (
                lax.dot_general(wt[0, rows, :], geno[0], LANES_TO_LANES, preferred_element_type=F32)
                + lax.dot_general(wt[1, rows, :], geno[1], LANES_TO_LANES, preferred_element_type=F32)
            ).astype(BF16)
            for dx in (1, 2, 3):
                xy_copy(b, dy, dx).start()

            @pl.when(dy > 0)
            def _():
                xy_copy(b, dy, 0).start()

    def z_copy(b, group):
        to_zh = lax.rem(zh + OFFSETS[b], 4)
        return remote(
            zs.at[b, group], zr.at[core, z], z_send.at[b, group], z_recv.at[core, z],
            at(plane, to_zh * 4 + group // 2, lax.rem(group, 2)),
        )

    mine = zl * 2 + core

    def reduce_plane(b):
        @pl.loop(1, 16)
        def _(step):
            xy_copy(b, step // 4, lax.rem(step, 4)).wait_recv()

        total = s[b, pl.ds(pl.multiple_of(plane * 160, 160), 160), :].astype(F32)
        for step in range(1, 16):
            total += r[b, step].astype(F32)
        for group in range(8):
            zs[b, group] = jnp.concatenate(
                [total[group * 20 : group * 20 + 20], jnp.zeros((4, 128), F32)], axis=0
            )
        if b == 0:
            zr[core, z] = zs[0, mine]

    def send_along(b):
        @pl.loop(0 if b else 1, 8)
        def _(step):
            z_copy(b, lax.rem(mine + step, 8)).start()

    multiply(0)
    for b in (1, 2):
        for k in range(2):
            dosage_copy(b, k).wait_send()
    for k in range(2):
        dosage_copy(3, k).start()
    for b in (1, 2, 3):
        gram_copy(b).wait_recv()
    inverse = inverse_factor(unpack(gl[...] + gr[1] + gr[2] + gr[3]))
    qt[...] = jnp.zeros_like(qt)
    qt[0:24, :] = jnp.dot(inverse, design[...], precision=HI, preferred_element_type=F32)
    multiply(1)
    multiply(2)
    reduce_plane(0)
    reduce_plane(1)
    multiply(3)
    send_along(0)
    send_along(1)
    reduce_plane(2)
    send_along(2)
    reduce_plane(3)
    send_along(3)

    @pl.loop(1, 32)
    def _(step):
        other = lax.rem(z * 2 + core + step, 32)
        z_from, core_from = other // 2, lax.rem(other, 2)
        remote(
            zs.at[0, 0], zr.at[core_from, z_from], z_send.at[0, 0],
            z_recv.at[core_from, z_from], at(plane, z, 1 - core),
        ).wait_recv()

    raw = []
    for half in range(2):
        total = zr[half, 0]
        for source in range(1, 16):
            total += zr[half, source]
        raw.append(total)
    cross = jnp.zeros((24, 128), F32)
    squares = jnp.zeros((24, 1), F32)
    for half in range(2):
        cross += lax.dot_general(
            raw[half], qt[:, pl.ds(half * 128, 128)], LANES_TO_LANES, precision=HI,
            preferred_element_type=F32,
        )
        squares += jnp.sum(raw[half] * raw[half], axis=1, keepdims=True)
    st[...] = pack(jnp.where(lane == 24, squares, cross))
    for b in (3, 1, 2):
        stat_copy(b).start()
    for b in (1, 2, 3):
        stat_copy(b).wait_recv()
    stats = unpack(st[...] + sr[1] + sr[2] + sr[3])
    cross = jnp.where(lane < 24, stats, 0.0)
    squares = jnp.sum(jnp.where(lane == 24, stats, 0.0) - cross * cross, axis=1, keepdims=True)
    spread = jnp.maximum(squares, 0.0) / 1023.0
    scale = 1.0 / jnp.sqrt(spread + 1e-06)
    for half in range(2):
        fitted = jnp.dot(
            cross, qt[:, pl.ds(half * 128, 128)], precision=HI, preferred_element_type=F32
        )
        out_ref[:, pl.ds(half * 128, 128)] = ((raw[half] - fitted) * scale)[0:20]

    weight_copy.wait_send()
    for b, k in pieces:
        totals_copy(b, k).wait_send()
    for b, k in ((0, 1), (3, 0), (3, 1)):
        dosage_copy(b, k).wait_send()
    for b in (1, 2, 3):
        gram_copy(b).wait_send()
        stat_copy(b).wait_send()
    for b in range(4):

        @pl.loop(1, 16)
        def _(step):
            xy_copy(b, step // 4, lax.rem(step, 4)).wait_send()

        @pl.loop(0 if b else 1, 8)
        def _(step):
            z_copy(b, lax.rem(mine + step, 8)).wait_send()


def on_device(dosages, weights, variant_pass, ancestry):
    dma = pltpu.SemaphoreType.DMA
    stay = pl.BlockSpec(memory_space=pltpu.HBM)
    return pl.pallas_call(
        kernel,
        out_shape=jax.ShapeDtypeStruct((20, 256), F32),
        in_specs=[stay] * 4,
        out_specs=pl.BlockSpec(memory_space=pltpu.VMEM),
        scratch_shapes=[
            pltpu.VMEM((256, 1024), jnp.int32),
            pltpu.VMEM((256, 2560), BF16),
            pltpu.VMEM((8, 128), jnp.int32),
            pltpu.VMEM((20, 256), F32),
            pltpu.VMEM((2, 2560, 256), BF16),
            pltpu.VMEM((4, 2, 128, 256), BF16),
            pltpu.VMEM((4, 2, 128, 256), BF16),
            pltpu.VMEM((4, 8, 128), F32),
            pltpu.VMEM((4, 2, 8, 128), F32),
            pltpu.VMEM((2, 2, 8, 128), F32),
            pltpu.VMEM((2, 128, 256), BF16),
            pltpu.VMEM((4, 2560, 128), BF16),
            pltpu.VMEM((4, 16, 160, 128), BF16),
            pltpu.VMEM((4, 8, 24, 128), F32),
            pltpu.VMEM((2, 16, 24, 128), F32),
            pltpu.VMEM((128, 256), F32),
            pltpu.VMEM((8, 128), F32),
            pltpu.VMEM((4, 8, 128), F32),
            pltpu.VMEM((128, 256), F32),
            pltpu.VMEM((8, 128), F32),
            pltpu.VMEM((4, 8, 128), F32),
            dma((4,)),
            dma((2,)),
            dma((4, 2)), dma((4, 2)), dma((4, 2)), dma((4, 2)),
            dma((4,)), dma((4,)),
            dma((4, 16)), dma((4, 16)),
            dma((4, 8)), dma((2, 16)),
            dma((4,)), dma((4,)),
        ],
        compiler_params=pltpu.CompilerParams(
            collective_id=0, has_side_effects=True, vmem_limit_bytes=64 << 20
        ),
        name="polygenic",
    )(dosages, weights, variant_pass.reshape(8, 128), ancestry.T)


def solution(mesh):
    in_specs = (P("samp", "var"), P(("var", "samp"), None), P("var"), P("samp", None))
    return jax.shard_map(
        on_device, mesh=mesh, in_specs=in_specs, out_specs=P("var", "samp"), check_vma=False
    )
```

```python
import jax
import jax.numpy as jnp
from jax import lax
from jax.experimental import pallas as pl
from jax.experimental.pallas import tpu as pltpu
from jax.sharding import PartitionSpec as P

F32 = jnp.float32
BF16 = jnp.bfloat16
HI = lax.Precision.HIGHEST
OFFSETS = (0, 1, 3, 2)
LANES_TO_LANES = (((1,), (1,)), ((), ()))


def pack(wide):
    return wide[0:8] + pltpu.roll(wide[8:16], 32, 1) + pltpu.roll(wide[16:24], 64, 1)


def unpack(tile):
    rows = jnp.concatenate([tile, pltpu.roll(tile, 96, 1), pltpu.roll(tile, 64, 1)], axis=0)
    return jnp.where(lax.broadcasted_iota(jnp.int32, (24, 128), 1) < 32, rows, 0.0)


def inverse_factor(gram):
    rows = lax.broadcasted_iota(jnp.int32, gram.shape, 0)
    lanes = lax.broadcasted_iota(jnp.int32, gram.shape, 1)
    work = jnp.where(lanes < 21, gram, 0.0) + jnp.where(lanes == rows + 64, 1.0, 0.0)
    for k in range(21):
        scale = 1.0 / jnp.sqrt(work[k : k + 1, k : k + 1])
        row = work[k : k + 1, :] * scale
        column = work[:, k : k + 1] * scale
        work = jnp.where(rows > k, work - column * row, jnp.where(rows == k, row, work))
    return jnp.where(lanes >= 64, work, 0.0)


def kernel(
    dos_hbm, w_hbm, pass_hbm, anc_hbm, out_ref,
    dos_ref, w_ref, pass_ref, anc_ref,
    wt, ds, dr, ts, tr, vec, geno, s, r, zs, zr, zsn, zrn, design, gl, gr, qt, st, sr,
    in_sem, w_sem, d_send, d_recv, t_send, t_recv, g_send, g_recv, xy_send, xy_recv, z_send, z_recv, zn_recv,
    st_send, st_recv,
):
    v, zh = lax.axis_index("var"), lax.axis_index("samp")
    core, zl = lax.rem(v, 2), lax.rem(v // 2, 4)
    x, y = lax.rem(v // 8, 4), v // 32
    z = zh * 4 + zl
    plane = y * 4 + x

    def at(plane_to, z_to, core_to):
        return {"var": (plane_to * 4 + lax.rem(z_to, 4)) * 2 + core_to, "samp": z_to // 4}

    def remote(src, dst, send, recv, to):
        return pltpu.make_async_remote_copy(
            src_ref=src, dst_ref=dst, send_sem=send, recv_sem=recv,
            device_id=to, device_id_type=pl.DeviceIdType.MESH,
        )

    loads = [
        pltpu.make_async_copy(src, dst, in_sem.at[i])
        for i, (src, dst) in enumerate(
            ((dos_hbm, dos_ref), (pass_hbm, pass_ref), (anc_hbm, anc_ref), (w_hbm, w_ref))
        )
    ]
    for load in loads:
        load.start()
    barrier = pltpu.get_barrier_semaphore()

    @pl.loop(1, 16)
    def _(step):
        pl.semaphore_signal(
            barrier, inc=1, device_id=at(lax.rem(plane + step, 16), z, core),
            device_id_type=pl.DeviceIdType.MESH,
        )

    @pl.loop(1, 32)
    def _(step):
        other = lax.rem(z * 2 + core + step, 32)
        pl.semaphore_signal(
            barrier, inc=1, device_id=at(plane, other // 2, lax.rem(other, 2)),
            device_id_type=pl.DeviceIdType.MESH,
        )

    loads[0].wait()
    loads[1].wait()
    for part in range(4):
        tile = []
        for half in range(2):
            piece = dos_ref[:, pl.ds(part * 256 + half * 128, 128)]
            seen = piece < 3
            tile.append(
                (
                    jnp.sum(jnp.where(seen, piece, 0), axis=0, keepdims=True).astype(F32),
                    jnp.sum(seen.astype(jnp.int32), axis=0, keepdims=True).astype(F32),
                )
            )
            narrow = piece.astype(F32).astype(BF16)
            for upper in range(2):
                ds[part, upper, :, pl.ds(half * 128, 128)] = narrow[upper * 128 : upper * 128 + 128]
        for half in range(2):
            ts[part, half : half + 1, :] = tile[half][0]
            ts[part, 2 + half : 3 + half, :] = tile[half][1]
            ts[part, 4 + half : 5 + half, :] = pass_ref[
                2 * part + half : 2 * part + half + 1, :
            ].astype(F32)
            ts[part, 6 + half : 7 + half, :] = jnp.zeros((1, 128), F32)
    loads[2].wait()
    design[...] = jnp.zeros_like(design)
    for row in (0, 64):
        design[row : row + 20, :] = anc_ref[...]
        design[row + 20 : row + 21, :] = jnp.ones((1, 256), F32)
    lane = lax.broadcasted_iota(jnp.int32, (24, 128), 1)
    gram = lax.dot_general(
        design[0:24, :], design[...], LANES_TO_LANES, precision=HI, preferred_element_type=F32
    )
    gl[...] = pack(jnp.where(lane < 32, gram, 0.0))
    loads[3].wait()
    for column in range(10):
        wt[0, pl.ds(column * 256, 256), :] = w_ref[:, pl.ds(column * 256, 256)].T
    dr[0, 0] = ds[zh, core]
    tr[0, 0] = ts[zh]

    pl.semaphore_wait(barrier, 46)

    def totals_copy(b, k):
        to_zh, to_core = lax.rem(zh + 4 - OFFSETS[b], 4), lax.rem(core + k, 2)
        return remote(
            ts.at[to_zh], tr.at[b, k], t_send.at[b, k], t_recv.at[b, k],
            at(plane, to_zh * 4 + zl, to_core),
        )

    def dosage_copy(b, k):
        to_zh, to_core = lax.rem(zh + 4 - OFFSETS[b], 4), lax.rem(core + k, 2)
        return remote(
            ds.at[to_zh, to_core], dr.at[b, k], d_send.at[b, k], d_recv.at[b, k],
            at(plane, to_zh * 4 + zl, to_core),
        )

    def dosage_to(b, to_core):
        return dosage_copy(b, lax.rem(core + to_core, 2))

    def small_copy(b, src, dst, send, recv):
        to_zh = lax.rem(zh + 4 - OFFSETS[b], 4)
        return remote(src, dst.at[b], send.at[b], recv.at[b], at(plane, to_zh * 4 + zl, core))

    def gram_copy(b):
        return small_copy(b, gl, gr, g_send, g_recv)

    def stat_copy(b):
        return small_copy(b, st, sr, st_send, st_recv)

    pieces = [(b, k) for b in (3, 1, 2, 0) for k in range(2) if b or k]
    weight_copy = remote(wt.at[0], wt.at[1], w_sem.at[0], w_sem.at[1], at(plane, z, 1 - core))
    for b, k in pieces:
        totals_copy(b, k).start()
    dosage_copy(0, 1).start()
    weight_copy.start()
    for upper in range(2):
        for b in (1, 2):
            dosage_to(b, upper).start()
    for b in (1, 2, 3):
        gram_copy(b).start()

    for b, k in pieces:
        totals_copy(b, k).wait_recv()
    for k in range(2):
        total = tr[0, k] + tr[1, k] + tr[2, k] + tr[3, k]
        for half in range(2):
            impute = (total[half : half + 1] + 1.0) / (total[2 + half : 3 + half] + 1.0)
            impute = impute.astype(BF16).astype(F32)
            centre = jnp.floor(impute * 4.0 + 0.5) * 0.25
            passed = tr[0, k, 4 + half : 5 + half, :]
            vec[k, half, 0:1, :] = centre
            vec[k, half, 1:2, :] = (impute - centre) * passed
            vec[k, half, 2:3, :] = passed

    def xy_copy(b, dy, dx):
        to = lax.rem(y + dy, 4) * 4 + lax.rem(x + dx, 4)
        return remote(
            s.at[b, pl.ds(to * 160, 160)], r.at[b, dy * 4 + dx],
            xy_send.at[b, dy * 4 + dx], xy_recv.at[b, dy * 4 + dx], at(to, z, core),
        )

    def multiply(b):
        for k in range(2):
            if b or k:
                dosage_copy(b, k).wait_recv()
            for half in range(2):
                dose = dr[b, k, :, pl.ds(half * 128, 128)].astype(F32)
                centre, missing = vec[k, half, 0:1, :], vec[k, half, 1:2, :]
                passed = vec[k, half, 2:3, :]
                geno[k, :, pl.ds(half * 128, 128)] = jnp.where(
                    dose < 2.5, (dose - centre) * passed, missing
                ).astype(BF16)
        if b == 0:
            weight_copy.wait_recv()

        @pl.loop(0, 4)
        def _(dy):
            rows = pl.ds(pl.multiple_of(lax.rem(y + dy, 4) * 640, 640), 640)
            s[b, rows, :] = (
                lax.dot_general(wt[0, rows, :], geno[0], LANES_TO_LANES, preferred_element_type=F32)
                + lax.dot_general(wt[1, rows, :], geno[1], LANES_TO_LANES, preferred_element_type=F32)
            ).astype(BF16)
            for dx in (1, 2, 3):
                xy_copy(b, dy, dx).start()

            @pl.when(dy > 0)
            def _():
                xy_copy(b, dy, 0).start()

    def z_copy(b, group):
        to_zh = lax.rem(zh + OFFSETS[b], 4)
        if b == 3:
            src, dst, arrived = zsn.at[group], zrn.at[core, zl], zn_recv.at[core, zl]
        else:
            src, dst, arrived = zs.at[b, group], zr.at[core, z], z_recv.at[core, z]
        return remote(
            src, dst, z_send.at[b, group], arrived,
            at(plane, to_zh * 4 + group // 2, lax.rem(group, 2)),
        )

    mine = zl * 2 + core

    def reduce_plane(b):
        @pl.loop(1, 16)
        def _(step):
            xy_copy(b, step // 4, lax.rem(step, 4)).wait_recv()

        total = s[b, pl.ds(pl.multiple_of(plane * 160, 160), 160), :].astype(F32)
        for step in range(1, 16):
            total += r[b, step].astype(F32)
        for group in range(8):
            part = jnp.concatenate(
                [total[group * 20 : group * 20 + 20], jnp.zeros((4, 128), F32)], axis=0
            )
            if b == 3:
                zsn[group] = part.astype(BF16)
            else:
                zs[b, group] = part
        if b == 0:
            zr[core, z] = zs[0, mine]

    def send_along(b):
        @pl.loop(0 if b else 1, 8)
        def _(step):
            z_copy(b, lax.rem(mine + step, 8)).start()

    multiply(0)
    for b in (1, 2):
        dosage_to(b, 0).wait_send()
    dosage_to(3, 0).start()
    for b in (1, 2):
        dosage_to(b, 1).wait_send()
    dosage_to(3, 1).start()
    for b in (1, 2, 3):
        gram_copy(b).wait_recv()
    inverse = inverse_factor(unpack(gl[...] + gr[1] + gr[2] + gr[3]))
    qt[...] = jnp.zeros_like(qt)
    qt[0:24, :] = jnp.dot(inverse, design[...], precision=HI, preferred_element_type=F32)
    multiply(1)
    multiply(2)
    reduce_plane(0)
    reduce_plane(1)
    multiply(3)
    send_along(0)
    send_along(1)
    reduce_plane(2)
    send_along(2)
    reduce_plane(3)
    send_along(3)

    for part in range(3):
        from_zh = lax.rem(zh + (0, 1, 3)[part], 4)

        @pl.loop(0 if part else 1, 8)
        def _(step):
            other = lax.rem(mine + step, 8)
            slot = (lax.rem(other, 2), from_zh * 4 + other // 2)
            remote(
                zs.at[0, 0], zr.at[slot], z_send.at[0, 0], z_recv.at[slot], at(plane, z, 1 - core)
            ).wait_recv()

    @pl.loop(0, 8)
    def _(other):
        slot = (lax.rem(other, 2), other // 2)
        remote(
            zsn.at[0], zrn.at[slot], z_send.at[0, 0], zn_recv.at[slot], at(plane, z, 1 - core)
        ).wait_recv()

    raw = []
    for half in range(2):
        total = zr[half, zh * 4]
        for source in range(1, 4):
            total += zr[half, zh * 4 + source]
        for shift in (1, 3):
            for source in range(4):
                total += zr[half, lax.rem(zh + shift, 4) * 4 + source]
        for source in range(4):
            total += zrn[half, source].astype(F32)
        raw.append(total)
    cross = jnp.zeros((24, 128), F32)
    squares = jnp.zeros((24, 1), F32)
    for half in range(2):
        cross += lax.dot_general(
            raw[half], qt[:, pl.ds(half * 128, 128)], LANES_TO_LANES, precision=HI,
            preferred_element_type=F32,
        )
        squares += jnp.sum(raw[half] * raw[half], axis=1, keepdims=True)
    st[...] = pack(jnp.where(lane == 24, squares, cross))
    for b in (3, 1, 2):
        stat_copy(b).start()
    for b in (1, 2, 3):
        stat_copy(b).wait_recv()
    stats = unpack(st[...] + sr[1] + sr[2] + sr[3])
    cross = jnp.where(lane < 24, stats, 0.0)
    squares = jnp.sum(jnp.where(lane == 24, stats, 0.0) - cross * cross, axis=1, keepdims=True)
    spread = jnp.maximum(squares, 0.0) / 1023.0
    scale = 1.0 / jnp.sqrt(spread + 1e-06)
    for half in range(2):
        fitted = jnp.dot(
            cross, qt[:, pl.ds(half * 128, 128)], precision=HI, preferred_element_type=F32
        )
        out_ref[:, pl.ds(half * 128, 128)] = ((raw[half] - fitted) * scale)[0:20]

    weight_copy.wait_send()
    for b, k in pieces:
        totals_copy(b, k).wait_send()
    for b, k in ((0, 1), (3, 0), (3, 1)):
        dosage_copy(b, k).wait_send()
    for b in (1, 2, 3):
        gram_copy(b).wait_send()
        stat_copy(b).wait_send()
    for b in range(4):

        @pl.loop(1, 16)
        def _(step):
            xy_copy(b, step // 4, lax.rem(step, 4)).wait_send()

        @pl.loop(0 if b else 1, 8)
        def _(step):
            z_copy(b, lax.rem(mine + step, 8)).wait_send()


def on_device(dosages, weights, variant_pass, ancestry):
    dma = pltpu.SemaphoreType.DMA
    stay = pl.BlockSpec(memory_space=pltpu.HBM)
    return pl.pallas_call(
        kernel,
        out_shape=jax.ShapeDtypeStruct((20, 256), F32),
        in_specs=[stay] * 4,
        out_specs=pl.BlockSpec(memory_space=pltpu.VMEM),
        scratch_shapes=[
            pltpu.VMEM((256, 1024), jnp.int32),
            pltpu.VMEM((256, 2560), BF16),
            pltpu.VMEM((8, 128), jnp.int32),
            pltpu.VMEM((20, 256), F32),
            pltpu.VMEM((2, 2560, 256), BF16),
            pltpu.VMEM((4, 2, 128, 256), BF16),
            pltpu.VMEM((4, 2, 128, 256), BF16),
            pltpu.VMEM((4, 8, 128), F32),
            pltpu.VMEM((4, 2, 8, 128), F32),
            pltpu.VMEM((2, 2, 8, 128), F32),
            pltpu.VMEM((2, 128, 256), BF16),
            pltpu.VMEM((4, 2560, 128), BF16),
            pltpu.VMEM((4, 16, 160, 128), BF16),
            pltpu.VMEM((3, 8, 24, 128), F32),
            pltpu.VMEM((2, 16, 24, 128), F32),
            pltpu.VMEM((8, 24, 128), BF16),
            pltpu.VMEM((2, 4, 24, 128), BF16),
            pltpu.VMEM((128, 256), F32),
            pltpu.VMEM((8, 128), F32),
            pltpu.VMEM((4, 8, 128), F32),
            pltpu.VMEM((128, 256), F32),
            pltpu.VMEM((8, 128), F32),
            pltpu.VMEM((4, 8, 128), F32),
            dma((4,)),
            dma((2,)),
            dma((4, 2)), dma((4, 2)), dma((4, 2)), dma((4, 2)),
            dma((4,)), dma((4,)),
            dma((4, 16)), dma((4, 16)),
            dma((4, 8)), dma((2, 16)), dma((2, 4)),
            dma((4,)), dma((4,)),
        ],
        compiler_params=pltpu.CompilerParams(
            collective_id=0, has_side_effects=True, vmem_limit_bytes=40 << 20
        ),
        name="polygenic",
    )(*(
        pltpu.with_memory_space_constraint(array, pltpu.HBM)
        for array in (dosages, weights, variant_pass.reshape(8, 128), ancestry.T)
    ))


def solution(mesh):
    in_specs = (P("samp", "var"), P(("var", "samp"), None), P("var"), P("samp", None))
    return jax.shard_map(
        on_device, mesh=mesh, in_specs=in_specs, out_specs=P("var", "samp"), check_vma=False
    )
```

```python
import jax
import jax.numpy as jnp
from jax import lax
from jax.experimental import pallas as pl
from jax.experimental.pallas import tpu as pltpu
from jax.sharding import PartitionSpec as P

F32 = jnp.float32
BF16 = jnp.bfloat16
HI = lax.Precision.HIGHEST
OFFSETS = (0, 1, 3, 2)
LANES_TO_LANES = (((1,), (1,)), ((), ()))


def pack(wide):
    return wide[0:8] + pltpu.roll(wide[8:16], 32, 1) + pltpu.roll(wide[16:24], 64, 1)


def unpack(tile):
    rows = jnp.concatenate([tile, pltpu.roll(tile, 96, 1), pltpu.roll(tile, 64, 1)], axis=0)
    return jnp.where(lax.broadcasted_iota(jnp.int32, (24, 128), 1) < 32, rows, 0.0)


def inverse_factor(gram):
    rows = lax.broadcasted_iota(jnp.int32, gram.shape, 0)
    lanes = lax.broadcasted_iota(jnp.int32, gram.shape, 1)
    work = jnp.where(lanes < 21, gram, 0.0) + jnp.where(lanes == rows + 64, 1.0, 0.0)
    for k in range(21):
        scale = 1.0 / jnp.sqrt(work[k : k + 1, k : k + 1])
        row = work[k : k + 1, :] * scale
        column = work[:, k : k + 1] * scale
        work = jnp.where(rows > k, work - column * row, jnp.where(rows == k, row, work))
    return jnp.where(lanes >= 64, work, 0.0)


def kernel(
    dos_hbm, w_hbm, pass_hbm, anc_hbm, out_ref,
    dos_ref, w_ref, pass_ref, pass_other, anc_ref,
    wt, ds, dr, ts, tr, vec, geno, s, r, zs, zr, zsn, zrn, design, gl, gr, qt, st, sr,
    in_sem, p_sem, w_sem, d_send, d_recv, t_send, t_recv, g_send, g_recv, xy_send, xy_recv, z_send, z_recv, zn_recv,
    st_send, st_recv,
):
    v, zh = lax.axis_index("var"), lax.axis_index("samp")
    core, zl = lax.rem(v, 2), lax.rem(v // 2, 4)
    x, y = lax.rem(v // 8, 4), v // 32
    z = zh * 4 + zl
    plane = y * 4 + x

    def at(plane_to, z_to, core_to):
        return {"var": (plane_to * 4 + lax.rem(z_to, 4)) * 2 + core_to, "samp": z_to // 4}

    def remote(src, dst, send, recv, to):
        return pltpu.make_async_remote_copy(
            src_ref=src, dst_ref=dst, send_sem=send, recv_sem=recv,
            device_id=to, device_id_type=pl.DeviceIdType.MESH,
        )

    loads = [
        pltpu.make_async_copy(src, dst, in_sem.at[i])
        for i, (src, dst) in enumerate(
            ((dos_hbm, dos_ref), (pass_hbm, pass_ref), (anc_hbm, anc_ref), (w_hbm, w_ref))
        )
    ]
    for load in loads:
        load.start()
    barrier = pltpu.get_barrier_semaphore()

    @pl.loop(1, 16)
    def _(step):
        pl.semaphore_signal(
            barrier, inc=1, device_id=at(lax.rem(plane + step, 16), z, core),
            device_id_type=pl.DeviceIdType.MESH,
        )

    @pl.loop(1, 32)
    def _(step):
        other = lax.rem(z * 2 + core + step, 32)
        pl.semaphore_signal(
            barrier, inc=1, device_id=at(plane, other // 2, lax.rem(other, 2)),
            device_id_type=pl.DeviceIdType.MESH,
        )

    loads[0].wait()
    loads[1].wait()
    for part in range(4):
        tile = []
        for half in range(2):
            piece = dos_ref[:, pl.ds(part * 256 + half * 128, 128)]
            seen = piece < 3
            tile.append(
                (
                    jnp.sum(jnp.where(seen, piece, 0), axis=0, keepdims=True).astype(F32),
                    jnp.sum(seen.astype(jnp.int32), axis=0, keepdims=True).astype(F32),
                )
            )
            narrow = piece.astype(F32).astype(BF16)
            for upper in range(2):
                ds[part, upper, :, pl.ds(half * 128, 128)] = narrow[upper * 128 : upper * 128 + 128]
        for half in range(2):
            ts[part, half : half + 1, :] = tile[half][0]
            ts[part, 2 + half : 3 + half, :] = tile[half][1]
    loads[2].wait()
    design[...] = jnp.zeros_like(design)
    for row in (0, 64):
        design[row : row + 20, :] = anc_ref[...]
        design[row + 20 : row + 21, :] = jnp.ones((1, 256), F32)
    lane = lax.broadcasted_iota(jnp.int32, (24, 128), 1)
    gram = lax.dot_general(
        design[0:24, :], design[...], LANES_TO_LANES, precision=HI, preferred_element_type=F32
    )
    gl[...] = pack(jnp.where(lane < 32, gram, 0.0))
    loads[3].wait()
    for column in range(10):
        wt[0, pl.ds(column * 256, 256), :] = w_ref[:, pl.ds(column * 256, 256)].T
    dr[0, 0] = ds[zh, core]
    tr[0, 0] = ts[zh]

    pl.semaphore_wait(barrier, 46)

    def totals_copy(b, k):
        to_zh, to_core = lax.rem(zh + 4 - OFFSETS[b], 4), lax.rem(core + k, 2)
        return remote(
            ts.at[to_zh], tr.at[b, k], t_send.at[b, k], t_recv.at[b, k],
            at(plane, to_zh * 4 + zl, to_core),
        )

    def dosage_copy(b, k):
        to_zh, to_core = lax.rem(zh + 4 - OFFSETS[b], 4), lax.rem(core + k, 2)
        return remote(
            ds.at[to_zh, to_core], dr.at[b, k], d_send.at[b, k], d_recv.at[b, k],
            at(plane, to_zh * 4 + zl, to_core),
        )

    def dosage_to(b, to_core):
        return dosage_copy(b, lax.rem(core + to_core, 2))

    def small_copy(b, src, dst, send, recv):
        to_zh = lax.rem(zh + 4 - OFFSETS[b], 4)
        return remote(src, dst.at[b], send.at[b], recv.at[b], at(plane, to_zh * 4 + zl, core))

    def gram_copy(b):
        return small_copy(b, gl, gr, g_send, g_recv)

    def stat_copy(b):
        return small_copy(b, st, sr, st_send, st_recv)

    pieces = [(b, k) for b in (3, 1, 2, 0) for k in range(2) if b or k]
    pass_copy = remote(pass_ref, pass_other, p_sem.at[0], p_sem.at[1], at(plane, z, 1 - core))
    weight_copy = remote(wt.at[0], wt.at[1], w_sem.at[0], w_sem.at[1], at(plane, z, 1 - core))
    for b, k in pieces:
        totals_copy(b, k).start()
    pass_copy.start()
    dosage_copy(0, 1).start()
    weight_copy.start()
    for upper in range(2):
        for b in (1, 2):
            dosage_to(b, upper).start()

    for b, k in pieces:
        totals_copy(b, k).wait_recv()
    pass_copy.wait_recv()
    for k in range(2):
        total = tr[0, k] + tr[1, k] + tr[2, k] + tr[3, k]
        for half in range(2):
            impute = (total[half : half + 1] + 1.0) / (total[2 + half : 3 + half] + 1.0)
            impute = impute.astype(BF16).astype(F32)
            centre = jnp.floor(impute * 4.0 + 0.5) * 0.25
            passed = (pass_other if k else pass_ref)[pl.ds(2 * zh + half, 1), :].astype(F32)
            vec[k, half, 0:1, :] = centre
            vec[k, half, 1:2, :] = (impute - centre) * passed
            vec[k, half, 2:3, :] = passed

    def xy_copy(b, dy, dx):
        to = lax.rem(y + dy, 4) * 4 + lax.rem(x + dx, 4)
        return remote(
            s.at[b, pl.ds(to * 160, 160)], r.at[b, dy * 4 + dx],
            xy_send.at[b, dy * 4 + dx], xy_recv.at[b, dy * 4 + dx], at(to, z, core),
        )

    def multiply(b, arrived=None):
        for k in range(2):
            if b or k:
                dosage_copy(b, k).wait_recv()
            for half in range(2):
                dose = dr[b, k, :, pl.ds(half * 128, 128)].astype(F32)
                centre, missing = vec[k, half, 0:1, :], vec[k, half, 1:2, :]
                passed = vec[k, half, 2:3, :]
                geno[k, :, pl.ds(half * 128, 128)] = jnp.where(
                    dose < 2.5, (dose - centre) * passed, missing
                ).astype(BF16)
        if arrived is not None:
            arrived()
        if b == 0:
            weight_copy.wait_recv()

        @pl.loop(0, 4)
        def _(dy):
            rows = pl.ds(pl.multiple_of(lax.rem(y + dy, 4) * 640, 640), 640)
            s[b, rows, :] = (
                lax.dot_general(wt[0, rows, :], geno[0], LANES_TO_LANES, preferred_element_type=F32)
                + lax.dot_general(wt[1, rows, :], geno[1], LANES_TO_LANES, preferred_element_type=F32)
            ).astype(BF16)
            for dx in (1, 2, 3):
                xy_copy(b, dy, dx).start()

            @pl.when(dy > 0)
            def _():
                xy_copy(b, dy, 0).start()

    def z_copy(b, group):
        to_zh = lax.rem(zh + OFFSETS[b], 4)
        if b == 3:
            src, dst, arrived = zsn.at[group], zrn.at[core, zl], zn_recv.at[core, zl]
        else:
            src, dst, arrived = zs.at[b, group], zr.at[core, z], z_recv.at[core, z]
        return remote(
            src, dst, z_send.at[b, group], arrived,
            at(plane, to_zh * 4 + group // 2, lax.rem(group, 2)),
        )

    mine = zl * 2 + core

    def reduce_plane(b):
        @pl.loop(1, 16)
        def _(step):
            xy_copy(b, step // 4, lax.rem(step, 4)).wait_recv()

        total = s[b, pl.ds(pl.multiple_of(plane * 160, 160), 160), :].astype(F32)
        for step in range(1, 16):
            total += r[b, step].astype(F32)
        for group in range(8):
            part = jnp.concatenate(
                [total[group * 20 : group * 20 + 20], jnp.zeros((4, 128), F32)], axis=0
            )
            if b == 3:
                zsn[group] = part.astype(BF16)
            else:
                zs[b, group] = part
        if b == 0:
            zr[core, z] = zs[0, mine]

    def send_along(b):
        @pl.loop(0 if b else 1, 8)
        def _(step):
            z_copy(b, lax.rem(mine + step, 8)).start()

    multiply(0)
    dosage_to(3, 0).start()
    dosage_to(3, 1).start()
    for b in (1, 2, 3):
        gram_copy(b).start()
    multiply(1)
    multiply(2)
    reduce_plane(0)
    send_along(0)
    reduce_plane(1)
    multiply(3)
    send_along(1)
    reduce_plane(2)
    send_along(2)
    for b in (1, 2, 3):
        gram_copy(b).wait_recv()
    inverse = inverse_factor(unpack(gl[...] + gr[1] + gr[2] + gr[3]))
    qt[...] = jnp.zeros_like(qt)
    qt[0:24, :] = jnp.dot(inverse, design[...], precision=HI, preferred_element_type=F32)
    reduce_plane(3)
    send_along(3)

    for part in range(3):
        from_zh = lax.rem(zh + (0, 1, 3)[part], 4)

        @pl.loop(0 if part else 1, 8)
        def _(step):
            other = lax.rem(mine + step, 8)
            slot = (lax.rem(other, 2), from_zh * 4 + other // 2)
            remote(
                zs.at[0, 0], zr.at[slot], z_send.at[0, 0], z_recv.at[slot], at(plane, z, 1 - core)
            ).wait_recv()

    @pl.loop(0, 8)
    def _(other):
        slot = (lax.rem(other, 2), other // 2)
        remote(
            zsn.at[0], zrn.at[slot], z_send.at[0, 0], zn_recv.at[slot], at(plane, z, 1 - core)
        ).wait_recv()

    raw = []
    for half in range(2):
        total = zr[half, zh * 4]
        for source in range(1, 4):
            total += zr[half, zh * 4 + source]
        for shift in (1, 3):
            for source in range(4):
                total += zr[half, lax.rem(zh + shift, 4) * 4 + source]
        for source in range(4):
            total += zrn[half, source].astype(F32)
        raw.append(total)
    cross = jnp.zeros((24, 128), F32)
    squares = jnp.zeros((24, 1), F32)
    for half in range(2):
        cross += lax.dot_general(
            raw[half], qt[:, pl.ds(half * 128, 128)], LANES_TO_LANES, precision=HI,
            preferred_element_type=F32,
        )
        squares += jnp.sum(raw[half] * raw[half], axis=1, keepdims=True)
    st[...] = pack(jnp.where(lane == 24, squares, cross))
    for b in (3, 1, 2):
        stat_copy(b).start()
    for b in (1, 2, 3):
        stat_copy(b).wait_recv()
    stats = unpack(st[...] + sr[1] + sr[2] + sr[3])
    cross = jnp.where(lane < 24, stats, 0.0)
    squares = jnp.sum(jnp.where(lane == 24, stats, 0.0) - cross * cross, axis=1, keepdims=True)
    spread = jnp.maximum(squares, 0.0) / 1023.0
    scale = 1.0 / jnp.sqrt(spread + 1e-06)
    for half in range(2):
        fitted = jnp.dot(
            cross, qt[:, pl.ds(half * 128, 128)], precision=HI, preferred_element_type=F32
        )
        out_ref[:, pl.ds(half * 128, 128)] = ((raw[half] - fitted) * scale)[0:20]

    pass_copy.wait_send()
    weight_copy.wait_send()
    for b, k in pieces:
        totals_copy(b, k).wait_send()
    for b, k in pieces:
        dosage_copy(b, k).wait_send()
    for b in (1, 2, 3):
        gram_copy(b).wait_send()
        stat_copy(b).wait_send()
    for b in range(4):

        @pl.loop(1, 16)
        def _(step):
            xy_copy(b, step // 4, lax.rem(step, 4)).wait_send()

        @pl.loop(0 if b else 1, 8)
        def _(step):
            z_copy(b, lax.rem(mine + step, 8)).wait_send()


def on_device(dosages, weights, variant_pass, ancestry):
    dma = pltpu.SemaphoreType.DMA
    stay = pl.BlockSpec(memory_space=pltpu.HBM)
    return pl.pallas_call(
        kernel,
        out_shape=jax.ShapeDtypeStruct((20, 256), F32),
        in_specs=[stay] * 4,
        out_specs=pl.BlockSpec(memory_space=pltpu.VMEM),
        scratch_shapes=[
            pltpu.VMEM((256, 1024), jnp.int32),
            pltpu.VMEM((256, 2560), BF16),
            pltpu.VMEM((8, 128), jnp.int32),
            pltpu.VMEM((8, 128), jnp.int32),
            pltpu.VMEM((20, 256), F32),
            pltpu.VMEM((2, 2560, 256), BF16),
            pltpu.VMEM((4, 2, 128, 256), BF16),
            pltpu.VMEM((4, 2, 128, 256), BF16),
            pltpu.VMEM((4, 4, 128), F32),
            pltpu.VMEM((4, 2, 4, 128), F32),
            pltpu.VMEM((2, 2, 8, 128), F32),
            pltpu.VMEM((2, 128, 256), BF16),
            pltpu.VMEM((4, 2560, 128), BF16),
            pltpu.VMEM((4, 16, 160, 128), BF16),
            pltpu.VMEM((3, 8, 24, 128), F32),
            pltpu.VMEM((2, 16, 24, 128), F32),
            pltpu.VMEM((8, 24, 128), BF16),
            pltpu.VMEM((2, 4, 24, 128), BF16),
            pltpu.VMEM((128, 256), F32),
            pltpu.VMEM((8, 128), F32),
            pltpu.VMEM((4, 8, 128), F32),
            pltpu.VMEM((128, 256), F32),
            pltpu.VMEM((8, 128), F32),
            pltpu.VMEM((4, 8, 128), F32),
            dma((4,)),
            dma((2,)),
            dma((2,)),
            dma((4, 2)), dma((4, 2)), dma((4, 2)), dma((4, 2)),
            dma((4,)), dma((4,)),
            dma((4, 16)), dma((4, 16)),
            dma((4, 8)), dma((2, 16)), dma((2, 4)),
            dma((4,)), dma((4,)),
        ],
        compiler_params=pltpu.CompilerParams(
            collective_id=0, has_side_effects=True, vmem_limit_bytes=40 << 20
        ),
        name="polygenic",
    )(*(
        pltpu.with_memory_space_constraint(array, pltpu.HBM)
        for array in (dosages, weights, variant_pass.reshape(8, 128), ancestry.T)
    ))


def solution(mesh):
    in_specs = (P("samp", "var"), P(("var", "samp"), None), P("var"), P("samp", None))
    return jax.shard_map(
        on_device, mesh=mesh, in_specs=in_specs, out_specs=P("var", "samp"), check_vma=False
    )
```

```python
import jax
import jax.numpy as jnp
from jax import lax
from jax.experimental import pallas as pl
from jax.experimental.pallas import tpu as pltpu
from jax.sharding import PartitionSpec as P

F32 = jnp.float32
BF16 = jnp.bfloat16
HI = lax.Precision.HIGHEST
OFFSETS = (0, 1, 3, 2)
LANES_TO_LANES = (((1,), (1,)), ((), ()))


def pack(wide):
    return wide[0:8] + pltpu.roll(wide[8:16], 32, 1) + pltpu.roll(wide[16:24], 64, 1)


def unpack(tile):
    rows = jnp.concatenate([tile, pltpu.roll(tile, 96, 1), pltpu.roll(tile, 64, 1)], axis=0)
    return jnp.where(lax.broadcasted_iota(jnp.int32, (24, 128), 1) < 32, rows, 0.0)


def inverse_factor(gram):
    rows = lax.broadcasted_iota(jnp.int32, gram.shape, 0)
    lanes = lax.broadcasted_iota(jnp.int32, gram.shape, 1)
    work = jnp.where(lanes < 21, gram, 0.0) + jnp.where(lanes == rows + 64, 1.0, 0.0)
    for k in range(21):
        scale = 1.0 / jnp.sqrt(work[k : k + 1, k : k + 1])
        row = work[k : k + 1, :] * scale
        column = work[:, k : k + 1] * scale
        work = jnp.where(rows > k, work - column * row, jnp.where(rows == k, row, work))
    return jnp.where(lanes >= 64, work, 0.0)


def kernel(
    dos_hbm, w_hbm, pass_hbm, anc_hbm, out_ref,
    dos_ref, w_ref, pass_ref, pass_other, anc_ref,
    wt, ds, dr, ts, tr, vec, geno, s, r, zs, zr, zsn, zrn, design, gl, gr, qt, st, sr,
    in_sem, p_sem, w_sem, d_send, d_recv, t_send, t_recv, g_send, g_recv, xy_send, xy_recv, z_send, z_recv, zn_recv,
    st_send, st_recv,
):
    v, zh = lax.axis_index("var"), lax.axis_index("samp")
    core, zl = lax.rem(v, 2), lax.rem(v // 2, 4)
    x, y = lax.rem(v // 8, 4), v // 32
    z = zh * 4 + zl
    plane = y * 4 + x

    def at(plane_to, z_to, core_to):
        return {"var": (plane_to * 4 + lax.rem(z_to, 4)) * 2 + core_to, "samp": z_to // 4}

    def remote(src, dst, send, recv, to):
        return pltpu.make_async_remote_copy(
            src_ref=src, dst_ref=dst, send_sem=send, recv_sem=recv,
            device_id=to, device_id_type=pl.DeviceIdType.MESH,
        )

    loads = [
        pltpu.make_async_copy(src, dst, in_sem.at[i])
        for i, (src, dst) in enumerate(
            ((dos_hbm, dos_ref), (pass_hbm, pass_ref), (anc_hbm, anc_ref), (w_hbm, w_ref))
        )
    ]
    for load in loads:
        load.start()
    barrier = pltpu.get_barrier_semaphore()

    @pl.loop(1, 16)
    def _(step):
        pl.semaphore_signal(
            barrier, inc=1, device_id=at(lax.rem(plane + step, 16), z, core),
            device_id_type=pl.DeviceIdType.MESH,
        )

    @pl.loop(1, 32)
    def _(step):
        other = lax.rem(z * 2 + core + step, 32)
        pl.semaphore_signal(
            barrier, inc=1, device_id=at(plane, other // 2, lax.rem(other, 2)),
            device_id_type=pl.DeviceIdType.MESH,
        )

    loads[0].wait()
    loads[1].wait()
    for part in range(4):
        tile = []
        for half in range(2):
            piece = dos_ref[:, pl.ds(part * 256 + half * 128, 128)]
            seen = piece < 3
            tile.append(
                (
                    jnp.sum(jnp.where(seen, piece, 0), axis=0, keepdims=True).astype(F32),
                    jnp.sum(seen.astype(jnp.int32), axis=0, keepdims=True).astype(F32),
                )
            )
            narrow = piece.astype(F32).astype(BF16)
            for upper in range(2):
                ds[part, upper, :, pl.ds(half * 128, 128)] = narrow[upper * 128 : upper * 128 + 128]
        for half in range(2):
            ts[part, half : half + 1, :] = tile[half][0]
            ts[part, 2 + half : 3 + half, :] = tile[half][1]
    loads[2].wait()
    design[...] = jnp.zeros_like(design)
    for row in (0, 64):
        design[row : row + 20, :] = anc_ref[...]
        design[row + 20 : row + 21, :] = jnp.ones((1, 256), F32)
    lane = lax.broadcasted_iota(jnp.int32, (24, 128), 1)
    gram = lax.dot_general(
        design[0:24, :], design[...], LANES_TO_LANES, precision=HI, preferred_element_type=F32
    )
    gl[...] = pack(jnp.where(lane < 32, gram, 0.0))
    loads[3].wait()
    for column in range(10):
        wt[0, pl.ds(column * 256, 256), :] = w_ref[:, pl.ds(column * 256, 256)].T
    dr[0, 0] = ds[zh, core]
    tr[0, 0] = ts[zh]

    pl.semaphore_wait(barrier, 46)

    def totals_copy(b, k):
        to_zh, to_core = lax.rem(zh + 4 - OFFSETS[b], 4), lax.rem(core + k, 2)
        return remote(
            ts.at[to_zh], tr.at[b, k], t_send.at[b, k], t_recv.at[b, k],
            at(plane, to_zh * 4 + zl, to_core),
        )

    def dosage_copy(b, k):
        to_zh, to_core = lax.rem(zh + 4 - OFFSETS[b], 4), lax.rem(core + k, 2)
        return remote(
            ds.at[to_zh, to_core], dr.at[b, k], d_send.at[b, k], d_recv.at[b, k],
            at(plane, to_zh * 4 + zl, to_core),
        )

    def dosage_to(b, to_core):
        return dosage_copy(b, lax.rem(core + to_core, 2))

    def small_copy(b, src, dst, send, recv):
        to_zh = lax.rem(zh + 4 - OFFSETS[b], 4)
        return remote(src, dst.at[b], send.at[b], recv.at[b], at(plane, to_zh * 4 + zl, core))

    def gram_copy(b):
        return small_copy(b, gl, gr, g_send, g_recv)

    def stat_copy(b):
        return small_copy(b, st, sr, st_send, st_recv)

    pieces = [(b, k) for b in (3, 1, 2, 0) for k in range(2) if b or k]
    pass_copy = remote(pass_ref, pass_other, p_sem.at[0], p_sem.at[1], at(plane, z, 1 - core))
    weight_copy = remote(wt.at[0], wt.at[1], w_sem.at[0], w_sem.at[1], at(plane, z, 1 - core))
    for b, k in pieces:
        totals_copy(b, k).start()
    pass_copy.start()
    dosage_copy(0, 1).start()
    weight_copy.start()
    for b in (1, 2, 3):
        dosage_to(b, 0).start()

    for b, k in pieces:
        totals_copy(b, k).wait_recv()
    pass_copy.wait_recv()
    for k in range(2):
        total = tr[0, k] + tr[1, k] + tr[2, k] + tr[3, k]
        for half in range(2):
            impute = (total[half : half + 1] + 1.0) / (total[2 + half : 3 + half] + 1.0)
            impute = impute.astype(BF16).astype(F32)
            centre = jnp.floor(impute * 4.0 + 0.5) * 0.25
            passed = (pass_other if k else pass_ref)[pl.ds(2 * zh + half, 1), :].astype(F32)
            vec[k, half, 0:1, :] = centre
            vec[k, half, 1:2, :] = (impute - centre) * passed
            vec[k, half, 2:3, :] = passed

    def xy_copy(b, dy, dx):
        to = lax.rem(y + dy, 4) * 4 + lax.rem(x + dx, 4)
        return remote(
            s.at[b, pl.ds(to * 160, 160)], r.at[b, dy * 4 + dx],
            xy_send.at[b, dy * 4 + dx], xy_recv.at[b, dy * 4 + dx], at(to, z, core),
        )

    def multiply(b, arrived=None):
        for k in range(2):
            if b or k:
                dosage_copy(b, k).wait_recv()
            for half in range(2):
                dose = dr[b, k, :, pl.ds(half * 128, 128)].astype(F32)
                centre, missing = vec[k, half, 0:1, :], vec[k, half, 1:2, :]
                passed = vec[k, half, 2:3, :]
                geno[k, :, pl.ds(half * 128, 128)] = jnp.where(
                    dose < 2.5, (dose - centre) * passed, missing
                ).astype(BF16)
        if arrived is not None:
            arrived()
        if b == 0:
            weight_copy.wait_recv()

        @pl.loop(0, 4)
        def _(dy):
            rows = pl.ds(pl.multiple_of(lax.rem(y + dy, 4) * 640, 640), 640)
            s[b, rows, :] = (
                lax.dot_general(wt[0, rows, :], geno[0], LANES_TO_LANES, preferred_element_type=F32)
                + lax.dot_general(wt[1, rows, :], geno[1], LANES_TO_LANES, preferred_element_type=F32)
            ).astype(BF16)
            for dx in (1, 2, 3):
                xy_copy(b, dy, dx).start()

            @pl.when(dy > 0)
            def _():
                xy_copy(b, dy, 0).start()

    def z_copy(b, group):
        to_zh = lax.rem(zh + OFFSETS[b], 4)
        if b == 3:
            src, dst, arrived = zsn.at[group], zrn.at[core, zl], zn_recv.at[core, zl]
        else:
            src, dst, arrived = zs.at[b, group], zr.at[core, z], z_recv.at[core, z]
        return remote(
            src, dst, z_send.at[b, group], arrived,
            at(plane, to_zh * 4 + group // 2, lax.rem(group, 2)),
        )

    mine = zl * 2 + core

    def reduce_plane(b):
        total = s[b, pl.ds(pl.multiple_of(plane * 160, 160), 160), :].astype(F32)
        for step in (1, 3, 4, 12, 2, 8, 5, 7, 13, 15, 6, 9, 11, 14, 10):
            xy_copy(b, step // 4, step % 4).wait_recv()
            total += r[b, step].astype(F32)
        for group in range(8):
            part = jnp.concatenate(
                [total[group * 20 : group * 20 + 20], jnp.zeros((4, 128), F32)], axis=0
            )
            if b == 3:
                zsn[group] = part.astype(BF16)
            else:
                zs[b, group] = part
        if b == 0:
            zr[core, z] = zs[0, mine]

    def send_along(b):
        @pl.loop(0 if b else 1, 8)
        def _(step):
            z_copy(b, lax.rem(mine + step, 8)).start()

    for b in (1, 2):
        dosage_to(b, 1).start()
    multiply(0)
    dosage_to(3, 1).start()
    multiply(1)
    multiply(2)
    for b in (1, 2, 3):
        gram_copy(b).start()
    reduce_plane(0)
    send_along(0)
    reduce_plane(1)
    multiply(3)
    send_along(1)
    reduce_plane(2)
    send_along(2)
    for b in (1, 2, 3):
        gram_copy(b).wait_recv()
    inverse = inverse_factor(unpack(gl[...] + gr[1] + gr[2] + gr[3]))
    qt[...] = jnp.zeros_like(qt)
    qt[0:24, :] = jnp.dot(inverse, design[...], precision=HI, preferred_element_type=F32)
    reduce_plane(3)
    send_along(3)

    for part in range(3):
        from_zh = lax.rem(zh + (0, 1, 3)[part], 4)

        @pl.loop(0 if part else 1, 8)
        def _(step):
            other = lax.rem(mine + step, 8)
            slot = (lax.rem(other, 2), from_zh * 4 + other // 2)
            remote(
                zs.at[0, 0], zr.at[slot], z_send.at[0, 0], z_recv.at[slot], at(plane, z, 1 - core)
            ).wait_recv()

    raw = []
    for half in range(2):
        total = zr[half, zh * 4]
        for source in range(1, 4):
            total += zr[half, zh * 4 + source]
        for shift in (1, 3):
            for source in range(4):
                total += zr[half, lax.rem(zh + shift, 4) * 4 + source]
        raw.append(total)
    raw = jnp.concatenate(raw, axis=1)
    for source in range(4):
        for half in range(2):
            remote(
                zsn.at[0], zrn.at[half, source], z_send.at[0, 0], zn_recv.at[half, source],
                at(plane, z, 1 - core),
            ).wait_recv()
        raw += jnp.concatenate([zrn[0, source], zrn[1, source]], axis=1).astype(F32)
    cross = lax.dot_general(
        raw, qt[...], LANES_TO_LANES, precision=HI, preferred_element_type=F32
    )
    squares = jnp.sum(raw * raw, axis=1, keepdims=True)
    st[...] = pack(jnp.where(lane == 24, squares, cross))
    for b in (3, 1, 2):
        stat_copy(b).start()
    for b in (1, 2, 3):
        stat_copy(b).wait_recv()
    stats = unpack(st[...] + sr[1] + sr[2] + sr[3])
    cross = jnp.where(lane < 24, stats, 0.0)
    squares = jnp.sum(jnp.where(lane == 24, stats, 0.0) - cross * cross, axis=1, keepdims=True)
    spread = jnp.maximum(squares, 0.0) / 1023.0
    scale = 1.0 / jnp.sqrt(spread + 1e-06)
    fitted = jnp.dot(cross, qt[...], precision=HI, preferred_element_type=F32)
    out_ref[...] = ((raw - fitted) * scale)[0:20]

    pass_copy.wait_send()
    weight_copy.wait_send()
    for b, k in pieces:
        totals_copy(b, k).wait_send()
    for b, k in pieces:
        dosage_copy(b, k).wait_send()
    for b in (1, 2, 3):
        gram_copy(b).wait_send()
        stat_copy(b).wait_send()
    for b in range(4):

        @pl.loop(1, 16)
        def _(step):
            xy_copy(b, step // 4, lax.rem(step, 4)).wait_send()

        @pl.loop(0 if b else 1, 8)
        def _(step):
            z_copy(b, lax.rem(mine + step, 8)).wait_send()


def on_device(dosages, weights, variant_pass, ancestry):
    dma = pltpu.SemaphoreType.DMA
    stay = pl.BlockSpec(memory_space=pltpu.HBM)
    return pl.pallas_call(
        kernel,
        out_shape=jax.ShapeDtypeStruct((20, 256), F32),
        in_specs=[stay] * 4,
        out_specs=pl.BlockSpec(memory_space=pltpu.VMEM),
        scratch_shapes=[
            pltpu.VMEM((256, 1024), jnp.int32),
            pltpu.VMEM((256, 2560), BF16),
            pltpu.VMEM((8, 128), jnp.int32),
            pltpu.VMEM((8, 128), jnp.int32),
            pltpu.VMEM((20, 256), F32),
            pltpu.VMEM((2, 2560, 256), BF16),
            pltpu.VMEM((4, 2, 128, 256), BF16),
            pltpu.VMEM((4, 2, 128, 256), BF16),
            pltpu.VMEM((4, 4, 128), F32),
            pltpu.VMEM((4, 2, 4, 128), F32),
            pltpu.VMEM((2, 2, 8, 128), F32),
            pltpu.VMEM((2, 128, 256), BF16),
            pltpu.VMEM((4, 2560, 128), BF16),
            pltpu.VMEM((4, 16, 160, 128), BF16),
            pltpu.VMEM((3, 8, 24, 128), F32),
            pltpu.VMEM((2, 16, 24, 128), F32),
            pltpu.VMEM((8, 24, 128), BF16),
            pltpu.VMEM((2, 4, 24, 128), BF16),
            pltpu.VMEM((128, 256), F32),
            pltpu.VMEM((8, 128), F32),
            pltpu.VMEM((4, 8, 128), F32),
            pltpu.VMEM((128, 256), F32),
            pltpu.VMEM((8, 128), F32),
            pltpu.VMEM((4, 8, 128), F32),
            dma((4,)),
            dma((2,)),
            dma((2,)),
            dma((4, 2)), dma((4, 2)), dma((4, 2)), dma((4, 2)),
            dma((4,)), dma((4,)),
            dma((4, 16)), dma((4, 16)),
            dma((4, 8)), dma((2, 16)), dma((2, 4)),
            dma((4,)), dma((4,)),
        ],
        compiler_params=pltpu.CompilerParams(
            collective_id=0, has_side_effects=True, vmem_limit_bytes=40 << 20
        ),
        name="polygenic",
    )(*(
        pltpu.with_memory_space_constraint(array, pltpu.HBM)
        for array in (dosages, weights, variant_pass.reshape(8, 128), ancestry.T)
    ))


def solution(mesh):
    in_specs = (P("samp", "var"), P(("var", "samp"), None), P("var"), P("samp", None))
    return jax.shard_map(
        on_device, mesh=mesh, in_specs=in_specs, out_specs=P("var", "samp"), check_vma=False
    )
```

```python
import jax
import jax.numpy as jnp
from jax import lax
from jax.experimental import pallas as pl
from jax.experimental.pallas import tpu as pltpu
from jax.sharding import PartitionSpec as P

F32 = jnp.float32
BF16 = jnp.bfloat16
HI = lax.Precision.HIGHEST
OFFSETS = (0, 1, 3, 2)
LANES_TO_LANES = (((1,), (1,)), ((), ()))


def pack(wide):
    return wide[0:8] + pltpu.roll(wide[8:16], 32, 1) + pltpu.roll(wide[16:24], 64, 1)


def unpack(tile):
    rows = jnp.concatenate([tile, pltpu.roll(tile, 96, 1), pltpu.roll(tile, 64, 1)], axis=0)
    return jnp.where(lax.broadcasted_iota(jnp.int32, (24, 128), 1) < 32, rows, 0.0)


def inverse_factor(gram):
    rows = lax.broadcasted_iota(jnp.int32, gram.shape, 0)
    lanes = lax.broadcasted_iota(jnp.int32, gram.shape, 1)
    work = jnp.where(lanes < 21, gram, 0.0) + jnp.where(lanes == rows + 64, 1.0, 0.0)
    for k in range(21):
        scale = 1.0 / jnp.sqrt(work[k : k + 1, k : k + 1])
        row = work[k : k + 1, :] * scale
        column = work[:, k : k + 1] * scale
        work = jnp.where(rows > k, work - column * row, jnp.where(rows == k, row, work))
    return jnp.where(lanes >= 64, work, 0.0)


def kernel(
    dos_hbm, w_hbm, pass_hbm, anc_hbm, out_ref,
    dos_ref, w_ref, pass_ref, pass_other, anc_ref,
    wt, ds, dr, ts, tr, vec, geno, s, r, zs, zr, zsn, zrn, design, gl, gr, qt, st, sr,
    in_sem, p_sem, w_sem, d_send, d_recv, t_send, t_recv, g_send, g_recv, xy_send, xy_recv, z_send, z_recv, zn_recv,
    st_send, st_recv,
):
    v, zh = lax.axis_index("var"), lax.axis_index("samp")
    core, zl = lax.rem(v, 2), lax.rem(v // 2, 4)
    x, y = lax.rem(v // 8, 4), v // 32
    z = zh * 4 + zl
    plane = y * 4 + x

    def at(plane_to, z_to, core_to):
        return {"var": (plane_to * 4 + lax.rem(z_to, 4)) * 2 + core_to, "samp": z_to // 4}

    def remote(src, dst, send, recv, to):
        return pltpu.make_async_remote_copy(
            src_ref=src, dst_ref=dst, send_sem=send, recv_sem=recv,
            device_id=to, device_id_type=pl.DeviceIdType.MESH,
        )

    loads = [
        pltpu.make_async_copy(src, dst, in_sem.at[i])
        for i, (src, dst) in enumerate(
            ((dos_hbm, dos_ref), (pass_hbm, pass_ref), (anc_hbm, anc_ref), (w_hbm, w_ref))
        )
    ]
    for load in loads:
        load.start()
    barrier = pltpu.get_barrier_semaphore()

    @pl.loop(1, 16)
    def _(step):
        pl.semaphore_signal(
            barrier, inc=1, device_id=at(lax.rem(plane + step, 16), z, core),
            device_id_type=pl.DeviceIdType.MESH,
        )

    @pl.loop(1, 32)
    def _(step):
        other = lax.rem(z * 2 + core + step, 32)
        pl.semaphore_signal(
            barrier, inc=1, device_id=at(plane, other // 2, lax.rem(other, 2)),
            device_id_type=pl.DeviceIdType.MESH,
        )

    loads[0].wait()
    loads[1].wait()
    for part in range(4):
        tile = []
        for half in range(2):
            piece = dos_ref[:, pl.ds(part * 256 + half * 128, 128)]
            seen = piece < 3
            tile.append(
                (
                    jnp.sum(jnp.where(seen, piece, 0), axis=0, keepdims=True).astype(F32),
                    jnp.sum(seen.astype(jnp.int32), axis=0, keepdims=True).astype(F32),
                )
            )
            narrow = piece.astype(F32).astype(BF16)
            for upper in range(2):
                ds[part, upper, :, pl.ds(half * 128, 128)] = narrow[upper * 128 : upper * 128 + 128]
        for half in range(2):
            ts[part, half : half + 1, :] = tile[half][0]
            ts[part, 2 + half : 3 + half, :] = tile[half][1]
    loads[2].wait()
    design[...] = jnp.zeros_like(design)
    for row in (0, 64):
        design[row : row + 20, :] = anc_ref[...]
        design[row + 20 : row + 21, :] = jnp.ones((1, 256), F32)
    lane = lax.broadcasted_iota(jnp.int32, (24, 128), 1)
    gram = lax.dot_general(
        design[0:24, :], design[...], LANES_TO_LANES, precision=HI, preferred_element_type=F32
    )
    gl[...] = pack(jnp.where(lane < 32, gram, 0.0))
    loads[3].wait()
    for column in range(10):
        wt[0, pl.ds(column * 256, 256), :] = w_ref[:, pl.ds(column * 256, 256)].T
    dr[0, 0] = ds[zh, core]
    tr[0, 0] = ts[zh]

    pl.semaphore_wait(barrier, 46)

    def totals_copy(b, k):
        to_zh, to_core = lax.rem(zh + 4 - OFFSETS[b], 4), lax.rem(core + k, 2)
        return remote(
            ts.at[to_zh], tr.at[b, k], t_send.at[b, k], t_recv.at[b, k],
            at(plane, to_zh * 4 + zl, to_core),
        )

    def dosage_copy(b, k):
        to_zh, to_core = lax.rem(zh + 4 - OFFSETS[b], 4), lax.rem(core + k, 2)
        return remote(
            ds.at[to_zh, to_core], dr.at[b, k], d_send.at[b, k], d_recv.at[b, k],
            at(plane, to_zh * 4 + zl, to_core),
        )

    def dosage_to(b, to_core):
        return dosage_copy(b, lax.rem(core + to_core, 2))

    def small_copy(b, src, dst, send, recv):
        to_zh = lax.rem(zh + 4 - OFFSETS[b], 4)
        return remote(src, dst.at[b], send.at[b], recv.at[b], at(plane, to_zh * 4 + zl, core))

    def gram_copy(b):
        return small_copy(b, gl, gr, g_send, g_recv)

    def stat_copy(b):
        return small_copy(b, st, sr, st_send, st_recv)

    pieces = [(b, k) for b in (3, 1, 2, 0) for k in range(2) if b or k]
    pass_copy = remote(pass_ref, pass_other, p_sem.at[0], p_sem.at[1], at(plane, z, 1 - core))
    weight_copy = remote(wt.at[0], wt.at[1], w_sem.at[0], w_sem.at[1], at(plane, z, 1 - core))
    for b, k in pieces:
        totals_copy(b, k).start()
    pass_copy.start()
    dosage_copy(0, 1).start()
    weight_copy.start()
    for b in (1, 2, 3):
        dosage_to(b, 0).start()

    for b, k in pieces:
        totals_copy(b, k).wait_recv()
    pass_copy.wait_recv()
    for k in range(2):
        total = tr[0, k] + tr[1, k] + tr[2, k] + tr[3, k]
        for half in range(2):
            impute = (total[half : half + 1] + 1.0) / (total[2 + half : 3 + half] + 1.0)
            impute = impute.astype(BF16).astype(F32)
            centre = jnp.floor(impute * 4.0 + 0.5) * 0.25
            passed = (pass_other if k else pass_ref)[pl.ds(2 * zh + half, 1), :].astype(F32)
            vec[k, half, 0:1, :] = centre
            vec[k, half, 1:2, :] = (impute - centre) * passed
            vec[k, half, 2:3, :] = passed

    def xy_copy(b, dy, dx):
        to = lax.rem(y + dy, 4) * 4 + lax.rem(x + dx, 4)
        return remote(
            s.at[b, pl.ds(to * 160, 160)], r.at[b, dy * 4 + dx],
            xy_send.at[b, dy * 4 + dx], xy_recv.at[b, dy * 4 + dx], at(to, z, core),
        )

    def multiply(b, arrived=None):
        for k in range(2):
            if b or k:
                dosage_copy(b, k).wait_recv()
            for half in range(2):
                dose = dr[b, k, :, pl.ds(half * 128, 128)].astype(F32)
                centre, missing = vec[k, half, 0:1, :], vec[k, half, 1:2, :]
                passed = vec[k, half, 2:3, :]
                geno[k, :, pl.ds(half * 128, 128)] = jnp.where(
                    dose < 2.5, (dose - centre) * passed, missing
                ).astype(BF16)
        if arrived is not None:
            arrived()
        if b == 0:
            weight_copy.wait_recv()

        @pl.loop(0, 4)
        def _(dy):
            rows = pl.ds(pl.multiple_of(lax.rem(y + dy, 4) * 640, 640), 640)
            s[b, rows, :] = (
                lax.dot_general(wt[0, rows, :], geno[0], LANES_TO_LANES, preferred_element_type=F32)
                + lax.dot_general(wt[1, rows, :], geno[1], LANES_TO_LANES, preferred_element_type=F32)
            ).astype(BF16)
            for dx in (1, 2, 3):
                xy_copy(b, dy, dx).start()

            @pl.when(dy > 0)
            def _():
                xy_copy(b, dy, 0).start()

    def z_copy(b, group):
        to_zh = lax.rem(zh + OFFSETS[b], 4)
        if b == 3:
            src, dst, arrived = zsn.at[group], zrn.at[core, zl], zn_recv.at[core, zl]
        else:
            src, dst, arrived = zs.at[b, group], zr.at[core, z], z_recv.at[core, z]
        return remote(
            src, dst, z_send.at[b, group], arrived,
            at(plane, to_zh * 4 + group // 2, lax.rem(group, 2)),
        )

    mine = zl * 2 + core

    def reduce_plane(b):
        total = s[b, pl.ds(pl.multiple_of(plane * 160, 160), 160), :].astype(F32)
        for step in (1, 3, 4, 12, 2, 8, 5, 7, 13, 15, 6, 9, 11, 14, 10):
            xy_copy(b, step // 4, step % 4).wait_recv()
            total += r[b, step].astype(F32)
        for group in range(8):
            part = jnp.concatenate(
                [total[group * 20 : group * 20 + 20], jnp.zeros((4, 128), F32)], axis=0
            )
            if b == 3:
                zsn[group] = part.astype(BF16)
            else:
                zs[b, group] = part
        if b == 0:
            zr[core, z] = zs[0, mine]

    def send_along(b):
        @pl.loop(0 if b else 1, 8)
        def _(step):
            z_copy(b, lax.rem(mine + step, 8)).start()

    for b in (1, 2):
        dosage_to(b, 1).start()
    multiply(0)
    dosage_to(3, 1).start()
    multiply(1)
    multiply(2)
    for b in (1, 2, 3):
        gram_copy(b).start()
    multiply(3)
    reduce_plane(0)
    send_along(0)
    reduce_plane(1)
    send_along(1)
    reduce_plane(2)
    send_along(2)
    for b in (1, 2, 3):
        gram_copy(b).wait_recv()
    inverse = inverse_factor(unpack(gl[...] + gr[1] + gr[2] + gr[3]))
    qt[...] = jnp.zeros_like(qt)
    qt[0:24, :] = jnp.dot(inverse, design[...], precision=HI, preferred_element_type=F32)
    reduce_plane(3)
    send_along(3)

    for part in range(3):
        from_zh = lax.rem(zh + (0, 1, 3)[part], 4)

        @pl.loop(0 if part else 1, 8)
        def _(step):
            other = lax.rem(mine + step, 8)
            slot = (lax.rem(other, 2), from_zh * 4 + other // 2)
            remote(
                zs.at[0, 0], zr.at[slot], z_send.at[0, 0], z_recv.at[slot], at(plane, z, 1 - core)
            ).wait_recv()

    raw = []
    for half in range(2):
        total = zr[half, zh * 4]
        for source in range(1, 4):
            total += zr[half, zh * 4 + source]
        for shift in (1, 3):
            for source in range(4):
                total += zr[half, lax.rem(zh + shift, 4) * 4 + source]
        raw.append(total)
    raw = jnp.concatenate(raw, axis=1)
    for source in range(4):
        for half in range(2):
            remote(
                zsn.at[0], zrn.at[half, source], z_send.at[0, 0], zn_recv.at[half, source],
                at(plane, z, 1 - core),
            ).wait_recv()
        raw += jnp.concatenate([zrn[0, source], zrn[1, source]], axis=1).astype(F32)
    cross = lax.dot_general(
        raw, qt[...], LANES_TO_LANES, precision=HI, preferred_element_type=F32
    )
    squares = jnp.sum(raw * raw, axis=1, keepdims=True)
    st[...] = pack(jnp.where(lane == 24, squares, cross))
    for b in (3, 1, 2):
        stat_copy(b).start()
    for b in (1, 2, 3):
        stat_copy(b).wait_recv()
    stats = unpack(st[...] + sr[1] + sr[2] + sr[3])
    cross = jnp.where(lane < 24, stats, 0.0)
    squares = jnp.sum(jnp.where(lane == 24, stats, 0.0) - cross * cross, axis=1, keepdims=True)
    spread = jnp.maximum(squares, 0.0) / 1023.0
    scale = 1.0 / jnp.sqrt(spread + 1e-06)
    fitted = jnp.dot(cross, qt[...], precision=HI, preferred_element_type=F32)
    out_ref[...] = ((raw - fitted) * scale)[0:20]

    pass_copy.wait_send()
    weight_copy.wait_send()
    for b, k in pieces:
        totals_copy(b, k).wait_send()
    for b, k in pieces:
        dosage_copy(b, k).wait_send()
    for b in (1, 2, 3):
        gram_copy(b).wait_send()
        stat_copy(b).wait_send()
    for b in range(4):

        @pl.loop(1, 16)
        def _(step):
            xy_copy(b, step // 4, lax.rem(step, 4)).wait_send()

        @pl.loop(0 if b else 1, 8)
        def _(step):
            z_copy(b, lax.rem(mine + step, 8)).wait_send()


def on_device(dosages, weights, variant_pass, ancestry):
    dma = pltpu.SemaphoreType.DMA
    stay = pl.BlockSpec(memory_space=pltpu.HBM)
    return pl.pallas_call(
        kernel,
        out_shape=jax.ShapeDtypeStruct((20, 256), F32),
        in_specs=[stay] * 4,
        out_specs=pl.BlockSpec(memory_space=pltpu.VMEM),
        scratch_shapes=[
            pltpu.VMEM((256, 1024), jnp.int32),
            pltpu.VMEM((256, 2560), BF16),
            pltpu.VMEM((8, 128), jnp.int32),
            pltpu.VMEM((8, 128), jnp.int32),
            pltpu.VMEM((20, 256), F32),
            pltpu.VMEM((2, 2560, 256), BF16),
            pltpu.VMEM((4, 2, 128, 256), BF16),
            pltpu.VMEM((4, 2, 128, 256), BF16),
            pltpu.VMEM((4, 4, 128), F32),
            pltpu.VMEM((4, 2, 4, 128), F32),
            pltpu.VMEM((2, 2, 8, 128), F32),
            pltpu.VMEM((2, 128, 256), BF16),
            pltpu.VMEM((4, 2560, 128), BF16),
            pltpu.VMEM((4, 16, 160, 128), BF16),
            pltpu.VMEM((3, 8, 24, 128), F32),
            pltpu.VMEM((2, 16, 24, 128), F32),
            pltpu.VMEM((8, 24, 128), BF16),
            pltpu.VMEM((2, 4, 24, 128), BF16),
            pltpu.VMEM((128, 256), F32),
            pltpu.VMEM((8, 128), F32),
            pltpu.VMEM((4, 8, 128), F32),
            pltpu.VMEM((128, 256), F32),
            pltpu.VMEM((8, 128), F32),
            pltpu.VMEM((4, 8, 128), F32),
            dma((4,)),
            dma((2,)),
            dma((2,)),
            dma((4, 2)), dma((4, 2)), dma((4, 2)), dma((4, 2)),
            dma((4,)), dma((4,)),
            dma((4, 16)), dma((4, 16)),
            dma((4, 8)), dma((2, 16)), dma((2, 4)),
            dma((4,)), dma((4,)),
        ],
        compiler_params=pltpu.CompilerParams(
            collective_id=0, has_side_effects=True, vmem_limit_bytes=40 << 20
        ),
        name="polygenic",
    )(*(
        pltpu.with_memory_space_constraint(array, pltpu.HBM)
        for array in (dosages, weights, variant_pass.reshape(8, 128), ancestry.T)
    ))


def solution(mesh):
    in_specs = (P("samp", "var"), P(("var", "samp"), None), P("var"), P("samp", None))
    return jax.shard_map(
        on_device, mesh=mesh, in_specs=in_specs, out_specs=P("var", "samp"), check_vma=False
    )
```
